256 devices in a mesh: zg: 16 (over z_lo, y, core), gx: 16 (over z_hi, x).
Axes of the slice: x: 4, y: 4, z: 8 (z_hi: 4, z_lo: 2; z = z_hi * 2 + z_lo), core: 2. Of those that a mesh axis runs over, the one named last changes fastest.
Arguments:
- observed: float32 [512, 1024, 256], P('zg', 'gx'), may hold values from 0.25 to 4
- kernel_x: float32 [33], replicated, may hold values from 0.2 to 1
- kernel_y: float32 [33], replicated, may hold values from 0.2 to 1
- kernel_z: float32 [65], replicated, may hold values from 0.2 to 1
Outputs:
- estimate: float32 [512, 1024, 256], P('zg', 'gx')
The draws below stay inside these ranges and needn't reach their ends.
All inputs are finite; a program needn't handle non-finite values.
Results may differ from the reference program's by a relative error of at most 0.0001.
Values sent between devices are 32-bit elements; how exact they have to be, the bound alone decides.
A program may use at most 64 MiB of HBM per device.

```python
import math
import jax
import jax.numpy as jnp
from jax import lax

KX = 33
KY = 33
KZ = 65
ITERS = 2
Y = 256
Z = 512
X = 1024


def level_of(rng, shape, pieces, least, largest):
    gain, own = 1.0, jax.random.fold_in(rng, 6)
    for position, blocks in pieces:
        heights = jnp.exp(jax.random.uniform(jax.random.fold_in(own, position), (blocks,), jnp.float32, least / len(pieces), largest / len(pieces)))
        gain = gain * jnp.repeat(heights, shape[position] // blocks).reshape([-1 if axis == position else 1 for axis in range(len(shape))])
    return gain


def setup_inputs(seed: int = 0) -> dict:
    streams_of = jax.random.split(jax.random.key(seed), 5)
    observed = jnp.clip(jnp.exp(math.log(4.0) - 2.7725887 * jax.random.uniform(streams_of[0], (Z, X, Y), jnp.float32) ** level_of(streams_of[0], (Z, X, Y), ((0, 16), (1, 16)), -0.2, 0.2)), 0.25, 4.0)
    kernel_x = jnp.clip(jnp.exp(jax.random.uniform(streams_of[1], (KX,), jnp.float32, math.log(0.2), math.log(1.0))), 0.2, 1.0)
    kernel_y = jnp.clip(jnp.exp(jax.random.uniform(streams_of[2], (KY,), jnp.float32, math.log(0.2), math.log(1.0))), 0.2, 1.0)
    kernel_z = jnp.clip(jnp.exp(jax.random.uniform(streams_of[3], (KZ,), jnp.float32, math.log(0.2), math.log(1.0))), 0.2, 1.0)
    return dict(observed=observed, kernel_x=kernel_x, kernel_y=kernel_y, kernel_z=kernel_z)


def band(prof, n_out, n_in, offset):
    diff = jnp.arange(n_in, dtype=jnp.int32)[None, :] - jnp.arange(n_out, dtype=jnp.int32)[:, None] + offset

    def add_tap(tap, acc):
        return acc + jnp.where(diff == tap, prof[tap], 0.0)

    return lax.fori_loop(0, prof.shape[0], add_tap, jnp.zeros((n_out, n_in), jnp.float32))


def apply_all(volume, mat_z, mat_x, mat_y):
    hp = lax.Precision.HIGHEST
    out = jnp.einsum('ij,zjy->ziy', mat_x, volume, precision=hp)
    out = jnp.einsum('zxj,ij->zxi', out, mat_y, precision=hp)
    return jnp.einsum('ij,jxy->ixy', mat_z, out, precision=hp)


def reference(observed, kernel_x, kernel_y, kernel_z):
    prof_x = kernel_x / jnp.sum(kernel_x)
    prof_y = kernel_y / jnp.sum(kernel_y)
    prof_z = kernel_z / jnp.sum(kernel_z)
    size_z, size_x, size_y = observed.shape
    half_x = (prof_x.shape[0] - 1) // 2
    half_y = (prof_y.shape[0] - 1) // 2
    half_z = (prof_z.shape[0] - 1) // 2
    fwd_x = band(prof_x, size_x, size_x, half_x)
    fwd_y = band(prof_y, size_y, size_y, half_y)
    fwd_z = band(prof_z, size_z, size_z, half_z)
    adj_x = band(prof_x[::-1], size_x, size_x, half_x)
    adj_y = band(prof_y[::-1], size_y, size_y, half_y)
    adj_z = band(prof_z[::-1], size_z, size_z, half_z)
    estimate = observed
    for step in range(ITERS):
        blurred = apply_all(estimate, fwd_z, fwd_x, fwd_y)
        ratio = observed / blurred
        correction = apply_all(ratio, adj_z, adj_x, adj_y)
        estimate = estimate * correction
    return estimate
```

```python
import functools

import jax
import jax.numpy as jnp
from jax import lax
from jax.experimental import pallas as pl
from jax.experimental.pallas import tpu as pltpu
from jax.sharding import PartitionSpec as P

STAGES = 4
CHUNKS = 4
MESH = pl.DeviceIdType.MESH
BF, F32 = jnp.bfloat16, jnp.float32


def split(v):
    hi = v.astype(BF)
    return hi, (v - hi.astype(F32)).astype(BF)


def mxu(a, b):
    return jnp.dot(a, b, preferred_element_type=F32)


def place(prof, width, step, start, rev):
    taps = prof.shape[1]
    h = prof / jnp.sum(prof)
    row = lax.broadcasted_iota(jnp.int32, (taps, width), 0)
    lane = lax.broadcasted_iota(jnp.int32, (taps, width), 1)
    t = (taps - 1 - row) if rev else row
    pick = jnp.where(lane == t * step + start, 1.0, 0.0).astype(F32)
    return lax.dot_general(
        jnp.broadcast_to(h, (8, taps)), pick, (((1,), (0,)), ((), ())),
        precision=lax.Precision.HIGHEST, preferred_element_type=F32,
    )[0:1]


def toeplitz(row, n):
    wide = jnp.broadcast_to(row, (n, row.shape[1]))
    return pltpu.roll(wide, 0, 1, stride=1, stride_axis=0)


def kernel(nz, nx, obs_ref, kx_ref, ky_ref, kz_ref, out_ref, comb, g, wz, wx, wyh, wyl,
           zsend, zrecv, xsend, xrecv):
    cols, slab, size_y = out_ref.shape
    part = cols // CHUNKS
    hz, hx = slab, part
    zg, gx = lax.axis_index("zg"), lax.axis_index("gx")
    odd = lax.rem(gx, 2)
    has_l, has_r = zg > 0, zg < nz - 1

    near = gx - 1 + 2 * odd
    far = gx + 1 - 2 * odd
    has_near = jnp.logical_and(gx > 0, gx < nx - 1)

    barrier = pltpu.get_barrier_semaphore()
    peers = (
        ((zg - 1, gx), has_l), ((zg + 1, gx), has_r), ((zg, near), has_near), ((zg, far), gx >= 0),
    )
    for peer, there in peers:
        @pl.when(there)
        def _():
            pl.semaphore_signal(barrier, inc=1, device_id=peer, device_id_type=MESH)

    def first(c):
        return part * (c + odd * (CHUNKS - 1 - 2 * c))

    def z_copy(s, c, side):
        rows = pl.ds(first(c), part)
        return pltpu.make_async_remote_copy(
            src_ref=comb.at[s, rows, pl.ds(hz, slab)],
            dst_ref=comb.at[s, rows, pl.ds((hz + slab) * (1 - side), slab)],
            send_sem=zsend.at[s, c, side], recv_sem=zrecv.at[s, c, side],
            device_id=(zg - 1 + 2 * side, gx), device_id_type=MESH,
        )

    def z_start(s, c):
        @pl.when(has_l)
        def _():
            z_copy(s, c, 0).start()

        @pl.when(has_r)
        def _():
            z_copy(s, c, 1).start()

    def x_copy(s, end):
        c = end * (CHUNKS - 1)
        low = (odd + end) % 2
        return pltpu.make_async_remote_copy(
            src_ref=g.at[s, pl.ds(hx + first(c), hx)],
            dst_ref=g.at[s, pl.ds((hx + cols) * (1 - low), hx)],
            send_sem=xsend.at[s, end], recv_sem=xrecv.at[s, end],
            device_id=(zg, near if end == 0 else far), device_id_type=MESH,
        )

    def z_pass(s, c):
        @pl.when(has_r)
        def _():
            z_copy(s, c, 0).wait_recv()

        @pl.when(has_l)
        def _():
            z_copy(s, c, 1).wait_recv()

        d = lax.rem(s, 2)
        both = wz[d]
        high = both[:slab]

        def column(i, _):
            hi, lo = split(comb[s, first(c) + i])
            top = mxu(both, hi)
            g[s, hx + first(c) + i] = top[:slab] + top[slab:] + mxu(high, lo)
            return 0

        lax.fori_loop(0, part, column, 0, unroll=4)
        if c == 0:
            @pl.when(has_near)
            def _():
                x_copy(s, 0).start()
        if c == CHUNKS - 1:
            x_copy(s, 1).start()

    def xy_pass(s, c):
        if c == 0:
            @pl.when(has_near)
            def _():
                x_copy(s, 0).wait_recv()
        if c == CHUNKS - 1:
            x_copy(s, 1).wait_recv()
        d = lax.rem(s, 2)
        rows = pl.ds(first(c), part)
        n = part * 8

        def group(k, _):
            zs = pl.ds(pl.multiple_of(k * 8, 8), 8)
            own = pl.ds(pl.multiple_of(hz + k * 8, 8), 8)
            hi, lo = split(g[s, pl.ds(first(c), part + 2 * hx), zs].reshape((part + 2 * hx) * 8, size_y))
            top = mxu(wx[d], hi)
            v = top[:n] + top[n:] + mxu(wx[d, :n], lo)
            hi, lo = split(v)
            v = mxu(hi, wyh[d]) + mxu(hi, wyl[d]) + mxu(lo, wyh[d])
            v = v.reshape(part, 8, size_y)

            @pl.when(d == 0)
            def _():
                comb[s + 1, rows, own] = comb[0, rows, own] / v

            @pl.when(s == 1)
            def _():
                comb[2, rows, own] = comb[0, rows, own] * v

            @pl.when(s == STAGES - 1)
            def _():
                out_ref[rows, zs] = comb[2, rows, own] * v

            return 0

        lax.fori_loop(0, slab // 8, group, 0)

        @pl.when(s < STAGES - 1)
        def _():
            z_start(s + 1, c)

    for c in range(CHUNKS):
        for x8 in range(0, part, 8):
            xs = pl.ds(pl.multiple_of(first(c) + x8, 8), 8)
            comb[0, xs, hz:hz + slab] = jnp.swapaxes(obs_ref[:, xs], 0, 1)
        if c == 0:
            pl.semaphore_wait(barrier, sum(there.astype(jnp.int32) for _, there in peers))
        z_start(0, c)

    for rev in (False, True):
        d = int(rev)
        hi, lo = split(toeplitz(place(kz_ref[...], 128, 1, 0, rev), slab)[:, :slab + 2 * hz])
        wz[d, :slab] = hi
        wz[d, slab:] = lo
        hi, lo = split(toeplitz(place(kx_ref[...], 8 * (part + 2 * hx), 8, 0, rev), part * 8))
        wx[d, :part * 8] = hi
        wx[d, part * 8:] = lo
        half = ky_ref.shape[1] // 2
        hi, lo = split(toeplitz(place(ky_ref[...], size_y + 256, 1, 128 - half, not rev), size_y)[:, 128:128 + size_y])
        wyh[d] = hi
        wyl[d] = lo

    def stage(s, _):
        zeros_z = jnp.zeros((1, hz, size_y), F32)
        zeros_x = jnp.zeros((1, slab, size_y), F32)

        def fill(there, ref, lo, n, zs, zeros):
            @pl.when(there)
            def _():
                def body(i, _):
                    ref[s, pl.ds(lo + i, 1), zs] = zeros
                    return 0
                lax.fori_loop(0, n, body, 0, unroll=4)

        fill(zg == 0, comb, 0, cols, pl.ds(0, hz), zeros_z)
        fill(zg == nz - 1, comb, 0, cols, pl.ds(hz + slab, hz), zeros_z)
        fill(gx == 0, g, 0, hx, pl.ds(0, slab), zeros_x)
        fill(gx == nx - 1, g, hx + cols, hx, pl.ds(0, slab), zeros_x)

        z_pass(s, 0)
        z_pass(s, 1)

        @pl.when(s > 0)
        def _():
            xy_pass(s - 1, CHUNKS - 1)

        z_pass(s, 2)
        xy_pass(s, 0)
        xy_pass(s, 1)
        z_pass(s, 3)
        xy_pass(s, 2)
        return 0

    lax.fori_loop(0, STAGES, stage, 0)
    xy_pass(STAGES - 1, CHUNKS - 1)

    def drain(s, _):
        for c in range(CHUNKS):
            @pl.when(has_l)
            def _():
                z_copy(s, c, 0).wait_send()

            @pl.when(has_r)
            def _():
                z_copy(s, c, 1).wait_send()

        @pl.when(has_near)
        def _():
            x_copy(s, 0).wait_send()

        x_copy(s, 1).wait_send()
        return 0

    lax.fori_loop(0, STAGES, drain, 0)


def shards(nz, nx, observed, kernel_x, kernel_y, kernel_z):
    slab, cols, size_y = observed.shape
    part = cols // CHUNKS
    wide = slab * 3
    out = pl.pallas_call(
        functools.partial(kernel, nz, nx),
        out_shape=jax.ShapeDtypeStruct((cols, slab, size_y), F32),
        in_specs=[pl.BlockSpec(memory_space=pltpu.VMEM)] * 4,
        out_specs=pl.BlockSpec(memory_space=pltpu.VMEM),
        scratch_shapes=[
            pltpu.VMEM((STAGES, cols, wide, size_y), F32),
            pltpu.VMEM((STAGES, cols + 2 * part, slab, size_y), F32),
            pltpu.VMEM((2, 2 * slab, wide), BF),
            pltpu.VMEM((2, 16 * part, 24 * part), BF),
            pltpu.VMEM((2, size_y, size_y), BF),
            pltpu.VMEM((2, size_y, size_y), BF),
            pltpu.SemaphoreType.DMA((STAGES, CHUNKS, 2)),
            pltpu.SemaphoreType.DMA((STAGES, CHUNKS, 2)),
            pltpu.SemaphoreType.DMA((STAGES, 2)),
            pltpu.SemaphoreType.DMA((STAGES, 2)),
        ],
        compiler_params=pltpu.CompilerParams(
            collective_id=0, has_side_effects=True, vmem_limit_bytes=56 * 2**20
        ),
        name="deconvolve",
    )(
        observed,
        kernel_x.reshape(1, -1), kernel_y.reshape(1, -1), kernel_z.reshape(1, -1),
    )
    return jnp.swapaxes(out, 0, 1)


def solution(mesh):
    return jax.shard_map(
        functools.partial(shards, mesh.shape["zg"], mesh.shape["gx"]),
        mesh=mesh,
        in_specs=(P("zg", "gx", None), P(), P(), P()),
        out_specs=P("zg", "gx", None),
        check_vma=False,
    )
```

```python
import functools

import jax
import jax.numpy as jnp
from jax import lax
from jax.experimental import pallas as pl
from jax.experimental.pallas import tpu as pltpu
from jax.sharding import PartitionSpec as P

STAGES = 4
CHUNKS = 4
RING = 4
Z_DIRECT, X_DIRECT = 8, 8
MESH = pl.DeviceIdType.MESH
BF, F32 = jnp.bfloat16, jnp.float32


def split(v):
    hi = v.astype(BF)
    return hi, (v - hi.astype(F32)).astype(BF)


def mxu(a, b):
    return jnp.dot(a, b, preferred_element_type=F32)


def place(prof, width, step, start, rev):
    taps = prof.shape[1]
    h = prof / jnp.sum(prof)
    row = lax.broadcasted_iota(jnp.int32, (taps, width), 0)
    lane = lax.broadcasted_iota(jnp.int32, (taps, width), 1)
    t = (taps - 1 - row) if rev else row
    pick = jnp.where(lane == t * step + start, 1.0, 0.0).astype(F32)
    return lax.dot_general(
        jnp.broadcast_to(h, (8, taps)), pick, (((1,), (0,)), ((), ())),
        precision=lax.Precision.HIGHEST, preferred_element_type=F32,
    )[0:1]


def toeplitz(row, n):
    wide = jnp.broadcast_to(row, (n, row.shape[1]))
    return pltpu.roll(wide, 0, 1, stride=1, stride_axis=0)


def kernel(nz, nx, obs_ref, kx_ref, ky_ref, kz_ref, out_ref, comb, g, zfw, xfw, wz, wx, wyh, wyl,
           zsend, zrecv, xsend, xrecv, zbsend, zbrecv, xbsend, xbrecv, xfsend, xfrecv):
    cols, slab, size_y = out_ref.shape
    part = cols // CHUNKS
    hz, hx = slab, part
    zg, gx = lax.axis_index("zg"), lax.axis_index("gx")
    odd = lax.rem(gx, 2)
    has_l, has_r = zg > 0, zg < nz - 1

    near = gx - 1 + 2 * odd
    far = gx + 1 - 2 * odd
    has_near = jnp.logical_and(gx > 0, gx < nx - 1)

    mid = nz // 2
    seam_l, seam_r = zg == mid, zg == mid - 1
    z_end = jnp.logical_or(zg == 0, zg == nz - 1)
    z_seam = jnp.logical_or(seam_l, seam_r)
    place_x = lax.rem(gx, RING)
    low_x, high_x = place_x == 0, place_x == RING - 1
    x_end = jnp.logical_or(low_x, high_x)
    turn = (1 - 2 * odd) * (RING - 1)
    over = RING * (1 - 2 * odd)
    x_seam = jnp.logical_and(x_end, has_near)
    x_forward = jnp.logical_and(x_end, jnp.logical_and(gx + over >= 0, gx + over < nx))
    x_from = jnp.logical_and(x_end, jnp.logical_and(gx - over >= 0, gx - over < nx))

    barrier = pltpu.get_barrier_semaphore()
    peers = (
        ((zg - 1, gx), has_l), ((zg + 1, gx), has_r), ((zg, near), has_near), ((zg, far), gx >= 0),
        ((jnp.where(z_end, mid, 0), gx), jnp.logical_or(z_end, z_seam)),
        ((jnp.where(z_end, mid - 1, nz - 1), gx), jnp.logical_or(z_end, z_seam)),
        ((zg, gx + turn), x_end), ((zg, gx + over), x_forward), ((zg, gx - over), x_from),
    )
    for peer, there in peers:
        @pl.when(there)
        def _():
            pl.semaphore_signal(barrier, inc=1, device_id=peer, device_id_type=MESH)

    def first(c):
        return part * (c + odd * (CHUNKS - 1 - 2 * c))

    def z_copy(s, c, side, n=part):
        rows = pl.ds(first(c), n)
        return pltpu.make_async_remote_copy(
            src_ref=comb.at[s, rows, pl.ds(hz, slab)],
            dst_ref=comb.at[s, rows, pl.ds((hz + slab) * (1 - side), slab)],
            send_sem=zsend.at[s, c, side], recv_sem=zrecv.at[s, c, side],
            device_id=(zg - 1 + 2 * side, gx), device_id_type=MESH,
        )

    def z_hop(s, c, side, hop):
        rows = pl.ds(first(c) + Z_DIRECT, part - Z_DIRECT)
        if hop == 0:
            src, dst, to = comb.at[s, rows, pl.ds(hz, slab)], zfw.at[s, c], (nz - 1) * (1 - side)
        else:
            src, dst, to = zfw.at[s, c], comb.at[s, rows, pl.ds((hz + slab) * (1 - side), slab)], mid - 1 + side
        return pltpu.make_async_remote_copy(
            src_ref=src, dst_ref=dst, send_sem=zbsend.at[s, c], recv_sem=zbrecv.at[s, c],
            device_id=(to, gx), device_id_type=MESH,
        )

    z_sides = ((0, has_l, seam_l, zg == nz - 1), (1, has_r, seam_r, zg == 0))

    def z_start(s, c):
        for side, there, seam, _ in z_sides:
            @pl.when(jnp.logical_and(there, jnp.logical_not(seam)))
            def _():
                z_copy(s, c, side).start()

            @pl.when(seam)
            def _():
                z_hop(s, c, side, 0).start()
                z_copy(s, c, side, Z_DIRECT).start()

    def z_sent(s, c):
        for side, there, seam, forwards in z_sides:
            @pl.when(jnp.logical_and(there, jnp.logical_not(seam)))
            def _():
                z_copy(s, c, side).wait_send()

            @pl.when(seam)
            def _():
                z_hop(s, c, side, 0).wait_send()
                z_copy(s, c, side, Z_DIRECT).wait_send()

            @pl.when(forwards)
            def _():
                z_hop(s, c, side, 1).wait_send()

    def z_arrived(s, c):
        for side, _, _, forwards in z_sides:
            @pl.when(forwards)
            def _():
                z_hop(s, c, side, 0).wait_recv()
                z_hop(s, c, side, 1).start()

        for side, there, seam in ((0, has_r, seam_r), (1, has_l, seam_l)):
            @pl.when(jnp.logical_and(there, jnp.logical_not(seam)))
            def _():
                z_copy(s, c, side).wait_recv()

            @pl.when(seam)
            def _():
                z_copy(s, c, side, Z_DIRECT).wait_recv()
                z_hop(s, c, side, 1).wait_recv()

    def x_hop(s, hop):
        if hop == 0:
            src, dst, to = g.at[s, pl.ds(hx + first(0) + X_DIRECT, hx - X_DIRECT)], xfw.at[s], gx + turn
            sems = xbsend, xfrecv
        else:
            src, dst, to = xfw.at[s], g.at[s, pl.ds((hx + cols) * odd + X_DIRECT, hx - X_DIRECT)], gx + over
            sems = xfsend, xbrecv
        return pltpu.make_async_remote_copy(
            src_ref=src, dst_ref=dst, send_sem=sems[0].at[s], recv_sem=sems[1].at[s],
            device_id=(zg, to), device_id_type=MESH,
        )

    def x_copy(s, end, n=part):
        c = end * (CHUNKS - 1)
        low = (odd + end) % 2
        return pltpu.make_async_remote_copy(
            src_ref=g.at[s, pl.ds(hx + first(c), n)],
            dst_ref=g.at[s, pl.ds((hx + cols) * (1 - low), n)],
            send_sem=xsend.at[s, end], recv_sem=xrecv.at[s, end],
            device_id=(zg, near if end == 0 else far), device_id_type=MESH,
        )

    def near_plain():
        return jnp.logical_and(has_near, jnp.logical_not(x_seam))

    def z_pass(s, c):
        z_arrived(s, c)
        d = lax.rem(s, 2)
        both = wz[d]
        high = both[:slab]

        def column(i, _):
            hi, lo = split(comb[s, first(c) + i])
            top = mxu(both, hi)
            g[s, hx + first(c) + i] = top[:slab] + top[slab:] + mxu(high, lo)
            return 0

        lax.fori_loop(0, part, column, 0, unroll=4)
        if c == 0:
            @pl.when(near_plain())
            def _():
                x_copy(s, 0).start()

            @pl.when(x_seam)
            def _():
                x_hop(s, 0).start()
                x_copy(s, 0, X_DIRECT).start()
        if c == CHUNKS - 1:
            x_copy(s, 1).start()

    def xy_pass(s, c):
        if c == 0:
            @pl.when(near_plain())
            def _():
                x_copy(s, 0).wait_recv()

            @pl.when(x_seam)
            def _():
                x_copy(s, 0, X_DIRECT).wait_recv()
                x_hop(s, 1).wait_recv()
        if c == CHUNKS - 1:
            x_copy(s, 1).wait_recv()
        d = lax.rem(s, 2)
        rows = pl.ds(first(c), part)
        n = part * 8

        def group(k, _):
            zs = pl.ds(pl.multiple_of(k * 8, 8), 8)
            own = pl.ds(pl.multiple_of(hz + k * 8, 8), 8)
            hi, lo = split(g[s, pl.ds(first(c), part + 2 * hx), zs].reshape((part + 2 * hx) * 8, size_y))
            top = mxu(wx[d], hi)
            v = top[:n] + top[n:] + mxu(wx[d, :n], lo)
            hi, lo = split(v)
            v = mxu(hi, wyh[d]) + mxu(hi, wyl[d]) + mxu(lo, wyh[d])
            v = v.reshape(part, 8, size_y)

            @pl.when(d == 0)
            def _():
                comb[s + 1, rows, own] = comb[0, rows, own] / v

            @pl.when(s == 1)
            def _():
                comb[2, rows, own] = comb[0, rows, own] * v

            @pl.when(s == STAGES - 1)
            def _():
                out_ref[rows, zs] = comb[2, rows, own] * v

            return 0

        lax.fori_loop(0, slab // 8, group, 0)

        @pl.when(s < STAGES - 1)
        def _():
            z_start(s + 1, c)

    for c in range(CHUNKS):
        for x8 in range(0, part, 8):
            xs = pl.ds(pl.multiple_of(first(c) + x8, 8), 8)
            comb[0, xs, hz:hz + slab] = jnp.swapaxes(obs_ref[:, xs], 0, 1)
        if c == 0:
            pl.semaphore_wait(barrier, sum(there.astype(jnp.int32) for _, there in peers))
        z_start(0, c)

    for rev in (False, True):
        d = int(rev)
        hi, lo = split(toeplitz(place(kz_ref[...], 128, 1, 0, rev), slab)[:, :slab + 2 * hz])
        wz[d, :slab] = hi
        wz[d, slab:] = lo
        hi, lo = split(toeplitz(place(kx_ref[...], 8 * (part + 2 * hx), 8, 0, rev), part * 8))
        wx[d, :part * 8] = hi
        wx[d, part * 8:] = lo
        half = ky_ref.shape[1] // 2
        hi, lo = split(toeplitz(place(ky_ref[...], size_y + 256, 1, 128 - half, not rev), size_y)[:, 128:128 + size_y])
        wyh[d] = hi
        wyl[d] = lo

    def stage(s, _):
        zeros_z = jnp.zeros((1, hz, size_y), F32)
        zeros_x = jnp.zeros((1, slab, size_y), F32)

        def fill(there, ref, lo, n, zs, zeros):
            @pl.when(there)
            def _():
                def body(i, _):
                    ref[s, pl.ds(lo + i, 1), zs] = zeros
                    return 0
                lax.fori_loop(0, n, body, 0, unroll=4)

        fill(zg == 0, comb, 0, cols, pl.ds(0, hz), zeros_z)
        fill(zg == nz - 1, comb, 0, cols, pl.ds(hz + slab, hz), zeros_z)
        fill(gx == 0, g, 0, hx, pl.ds(0, slab), zeros_x)
        fill(gx == nx - 1, g, hx + cols, hx, pl.ds(0, slab), zeros_x)

        z_pass(s, 0)
        z_pass(s, 1)

        @pl.when(x_forward)
        def _():
            x_hop(s, 0).wait_recv()
            x_hop(s, 1).start()

        @pl.when(s > 0)
        def _():
            xy_pass(s - 1, CHUNKS - 1)

        z_pass(s, 2)
        xy_pass(s, 0)
        xy_pass(s, 1)
        z_pass(s, 3)
        xy_pass(s, 2)
        return 0

    lax.fori_loop(0, STAGES, stage, 0)
    xy_pass(STAGES - 1, CHUNKS - 1)

    def drain(s, _):
        for c in range(CHUNKS):
            z_sent(s, c)

        @pl.when(near_plain())
        def _():
            x_copy(s, 0).wait_send()

        @pl.when(x_seam)
        def _():
            x_copy(s, 0, X_DIRECT).wait_send()
            x_hop(s, 0).wait_send()

        @pl.when(x_forward)
        def _():
            x_hop(s, 1).wait_send()

        x_copy(s, 1).wait_send()
        return 0

    lax.fori_loop(0, STAGES, drain, 0)


def shards(nz, nx, observed, kernel_x, kernel_y, kernel_z):
    slab, cols, size_y = observed.shape
    part = cols // CHUNKS
    wide = slab * 3
    out = pl.pallas_call(
        functools.partial(kernel, nz, nx),
        out_shape=jax.ShapeDtypeStruct((cols, slab, size_y), F32),
        in_specs=[pl.BlockSpec(memory_space=pltpu.VMEM)] * 4,
        out_specs=pl.BlockSpec(memory_space=pltpu.VMEM),
        scratch_shapes=[
            pltpu.VMEM((STAGES, cols, wide, size_y), F32),
            pltpu.VMEM((STAGES, cols + 2 * part, slab, size_y), F32),
            pltpu.VMEM((STAGES, CHUNKS, part - Z_DIRECT, slab, size_y), F32),
            pltpu.VMEM((STAGES, part - X_DIRECT, slab, size_y), F32),
            pltpu.VMEM((2, 2 * slab, wide), BF),
            pltpu.VMEM((2, 16 * part, 24 * part), BF),
            pltpu.VMEM((2, size_y, size_y), BF),
            pltpu.VMEM((2, size_y, size_y), BF),
            pltpu.SemaphoreType.DMA((STAGES, CHUNKS, 2)),
            pltpu.SemaphoreType.DMA((STAGES, CHUNKS, 2)),
            pltpu.SemaphoreType.DMA((STAGES, 2)),
            pltpu.SemaphoreType.DMA((STAGES, 2)),
            pltpu.SemaphoreType.DMA((STAGES, CHUNKS)),
            pltpu.SemaphoreType.DMA((STAGES, CHUNKS)),
            pltpu.SemaphoreType.DMA((STAGES,)),
            pltpu.SemaphoreType.DMA((STAGES,)),
            pltpu.SemaphoreType.DMA((STAGES,)),
            pltpu.SemaphoreType.DMA((STAGES,)),
        ],
        compiler_params=pltpu.CompilerParams(
            collective_id=0, has_side_effects=True, vmem_limit_bytes=56 * 2**20
        ),
        name="deconvolve",
    )(
        observed,
        kernel_x.reshape(1, -1), kernel_y.reshape(1, -1), kernel_z.reshape(1, -1),
    )
    return jnp.swapaxes(out, 0, 1)


def solution(mesh):
    return jax.shard_map(
        functools.partial(shards, mesh.shape["zg"], mesh.shape["gx"]),
        mesh=mesh,
        in_specs=(P("zg", "gx", None), P(), P(), P()),
        out_specs=P("zg", "gx", None),
        check_vma=False,
    )
```

```python
import functools

import jax
import jax.numpy as jnp
from jax import lax
from jax.experimental import pallas as pl
from jax.experimental.pallas import tpu as pltpu
from jax.sharding import PartitionSpec as P

STAGES = 4
CHUNKS = 4
PIECES = 8
PER = PIECES // CHUNKS
RING = 4
Z_DIRECT, X_DIRECT = 4, 5
MESH = pl.DeviceIdType.MESH
BF, F32 = jnp.bfloat16, jnp.float32


def split(v):
    hi = v.astype(BF)
    return hi, (v - hi.astype(F32)).astype(BF)


def mxu(a, b):
    return jnp.dot(a, b, preferred_element_type=F32)


def place(prof, width, step, start, rev):
    taps = prof.shape[1]
    h = prof / jnp.sum(prof)
    row = lax.broadcasted_iota(jnp.int32, (taps, width), 0)
    lane = lax.broadcasted_iota(jnp.int32, (taps, width), 1)
    t = (taps - 1 - row) if rev else row
    pick = jnp.where(lane == t * step + start, 1.0, 0.0).astype(F32)
    return lax.dot_general(
        jnp.broadcast_to(h, (8, taps)), pick, (((1,), (0,)), ((), ())),
        precision=lax.Precision.HIGHEST, preferred_element_type=F32,
    )[0:1]


def toeplitz(row, n):
    wide = jnp.broadcast_to(row, (n, row.shape[1]))
    return pltpu.roll(wide, 0, 1, stride=1, stride_axis=0)


def kernel(nz, nx, obs_ref, kx_ref, ky_ref, kz_ref, out_ref, comb, g, zfw, xfw, wz, wx, wyh, wyl,
           zsend, zrecv, xsend, xrecv, zbsend, zbrecv, xbsend, xbrecv, xfsend, xfrecv, xdone):
    slab, cols, size_y = out_ref.shape
    part, piece = cols // CHUNKS, cols // PIECES
    hz, hx = slab, part
    zg, gx = lax.axis_index("zg"), lax.axis_index("gx")
    odd = lax.rem(gx, 2)
    has_l, has_r = zg > 0, zg < nz - 1

    near = gx - 1 + 2 * odd
    far = gx + 1 - 2 * odd
    has_near = jnp.logical_and(gx > 0, gx < nx - 1)

    mid = nz // 2
    seam_l, seam_r = zg == mid, zg == mid - 1
    z_end = jnp.logical_or(zg == 0, zg == nz - 1)
    z_seam = jnp.logical_or(seam_l, seam_r)
    place_x = lax.rem(gx, RING)
    low_x, high_x = place_x == 0, place_x == RING - 1
    x_end = jnp.logical_or(low_x, high_x)
    turn = (1 - 2 * odd) * (RING - 1)
    over = RING * (1 - 2 * odd)
    x_seam = jnp.logical_and(x_end, has_near)
    x_forward = jnp.logical_and(x_end, jnp.logical_and(gx + over >= 0, gx + over < nx))
    x_from = jnp.logical_and(x_end, jnp.logical_and(gx - over >= 0, gx - over < nx))

    barrier = pltpu.get_barrier_semaphore()
    peers = (
        ((zg - 1, gx), has_l), ((zg + 1, gx), has_r), ((zg, near), has_near), ((zg, far), gx >= 0),
        ((jnp.where(z_end, mid, 0), gx), jnp.logical_or(z_end, z_seam)),
        ((jnp.where(z_end, mid - 1, nz - 1), gx), jnp.logical_or(z_end, z_seam)),
        ((zg, gx + turn), x_end), ((zg, gx + over), x_forward), ((zg, gx - over), x_from),
    )
    for peer, there in peers:
        @pl.when(there)
        def _():
            pl.semaphore_signal(barrier, inc=1, device_id=peer, device_id_type=MESH)

    def first(c):
        return part * (c + odd * (CHUNKS - 1 - 2 * c))

    def head(p):
        return piece * (p + odd * (PIECES - 1 - 2 * p))

    def z_copy(s, c, side, n=piece):
        rows = pl.ds(head(c), n)
        return pltpu.make_async_remote_copy(
            src_ref=comb.at[s, rows, pl.ds(hz, slab)],
            dst_ref=comb.at[s, rows, pl.ds((hz + slab) * (1 - side), slab)],
            send_sem=zsend.at[s, c, side], recv_sem=zrecv.at[s, c, side],
            device_id=(zg - 1 + 2 * side, gx), device_id_type=MESH,
        )

    def z_hop(s, c, side, hop):
        rows = pl.ds(head(c) + Z_DIRECT, piece - Z_DIRECT)
        if hop == 0:
            src, dst, to = comb.at[s, rows, pl.ds(hz, slab)], zfw.at[s, c], (nz - 1) * (1 - side)
        else:
            src, dst, to = zfw.at[s, c], comb.at[s, rows, pl.ds((hz + slab) * (1 - side), slab)], mid - 1 + side
        return pltpu.make_async_remote_copy(
            src_ref=src, dst_ref=dst, send_sem=zbsend.at[s, c], recv_sem=zbrecv.at[s, c],
            device_id=(to, gx), device_id_type=MESH,
        )

    z_sides = ((0, has_l, seam_l, zg == nz - 1), (1, has_r, seam_r, zg == 0))

    def z_start(s, c):
        for side, there, seam, _ in z_sides:
            @pl.when(jnp.logical_and(there, jnp.logical_not(seam)))
            def _():
                z_copy(s, c, side).start()

            @pl.when(seam)
            def _():
                z_hop(s, c, side, 0).start()
                z_copy(s, c, side, Z_DIRECT).start()

    def z_sent(s, c):
        for side, there, seam, forwards in z_sides:
            @pl.when(jnp.logical_and(there, jnp.logical_not(seam)))
            def _():
                z_copy(s, c, side).wait_send()

            @pl.when(seam)
            def _():
                z_hop(s, c, side, 0).wait_send()
                z_copy(s, c, side, Z_DIRECT).wait_send()

            @pl.when(forwards)
            def _():
                z_hop(s, c, side, 1).wait_send()

    def z_arrived(s, c):
        for side, _, _, forwards in z_sides:
            @pl.when(forwards)
            def _():
                z_hop(s, c, side, 0).wait_recv()
                z_hop(s, c, side, 1).start()

        for side, there, seam in ((0, has_r, seam_r), (1, has_l, seam_l)):
            @pl.when(jnp.logical_and(there, jnp.logical_not(seam)))
            def _():
                z_copy(s, c, side).wait_recv()

            @pl.when(seam)
            def _():
                z_copy(s, c, side, Z_DIRECT).wait_recv()
                z_hop(s, c, side, 1).wait_recv()

    def x_hop(s, p, hop):
        n = piece - X_DIRECT
        if hop == 0:
            src, dst, to = g.at[s, pl.ds(hx + head(p) + X_DIRECT, n)], xfw.at[s, p], gx + turn
            sems = xbsend, xfrecv
        else:
            at = (1 - odd) * (hx - piece * (p + 1)) + odd * (hx + cols + piece * p)
            src, dst, to = xfw.at[s, p], g.at[s, pl.ds(at + X_DIRECT, n)], gx + over
            sems = xfsend, xbrecv
        return pltpu.make_async_remote_copy(
            src_ref=src, dst_ref=dst, send_sem=sems[0].at[s, p], recv_sem=sems[1].at[s, p],
            device_id=(zg, to), device_id_type=MESH,
        )

    def x_copy(s, end, p, n=piece):
        at = head(p + end * (PIECES - PER))
        low = (odd + end) % 2
        to = at + (hx + cols) * (1 - low) - (cols - hx) * low
        return pltpu.make_async_remote_copy(
            src_ref=g.at[s, pl.ds(hx + at, n)],
            dst_ref=g.at[s, pl.ds(to, n)],
            send_sem=xsend.at[s, end, p], recv_sem=xrecv.at[s, end, p],
            device_id=(zg, near if end == 0 else far), device_id_type=MESH,
        )

    def near_plain():
        return jnp.logical_and(has_near, jnp.logical_not(x_seam))

    def x_forward_on(s, p):
        @pl.when(x_forward)
        def _():
            x_hop(s, p, 0).wait_recv()
            x_hop(s, p, 1).start()

    def z_pass(s, c):
        z_arrived(s, c)
        d = lax.rem(s, 2)
        both = wz[d]
        high = both[:slab]

        def column(i, _):
            hi, lo = split(comb[s, head(c) + i])
            top = mxu(both, hi)
            g[s, hx + head(c) + i] = top[:slab] + top[slab:] + mxu(high, lo)
            return 0

        lax.fori_loop(0, piece, column, 0, unroll=8)
        if c < PER:
            @pl.when(near_plain())
            def _():
                x_copy(s, 0, c).start()

            @pl.when(x_seam)
            def _():
                x_hop(s, c, 0).start()
                x_copy(s, 0, c, X_DIRECT).start()
        if c >= PIECES - PER:
            x_copy(s, 1, c - (PIECES - PER)).start()

    def xy_pass(s, c):
        if c == 0:
            for p in range(PER):
                @pl.when(near_plain())
                def _():
                    x_copy(s, 0, p).wait_recv()

                @pl.when(x_seam)
                def _():
                    x_copy(s, 0, p, X_DIRECT).wait_recv()
                    x_hop(s, p, 1).wait_recv()
        if c == CHUNKS - 1:
            for p in range(PER):
                x_copy(s, 1, p).wait_recv()
        d = lax.rem(s, 2)
        rows = pl.ds(first(c), part)
        n = part * 8

        def group(k, _):
            zs = pl.ds(pl.multiple_of(k * 8, 8), 8)
            hi, lo = split(g[s, pl.ds(first(c), part + 2 * hx), zs].reshape((part + 2 * hx) * 8, size_y))
            top = mxu(wx[d], hi)
            v = top[:n] + top[n:] + mxu(wx[d, :n], lo)
            xdone[:, zs] = v.reshape(part, 8, size_y)
            return 0

        lax.fori_loop(0, slab // 8, group, 0, unroll=4)
        hi, lo = split(xdone[...].reshape(part * slab, size_y))
        v = mxu(hi, wyh[d]) + mxu(lo, wyh[d]) + mxu(hi, wyl[d])
        v = v.reshape(part, slab, size_y)
        own = pl.ds(hz, slab)

        @pl.when(d == 0)
        def _():
            comb[s + 1, rows, own] = comb[0, rows, own] / v

        @pl.when(s == 1)
        def _():
            comb[2, rows, own] = comb[0, rows, own] * v

        @pl.when(s == STAGES - 1)
        def _():
            out_ref[:, pl.ds(pl.multiple_of(first(c), part), part)] = jnp.swapaxes(comb[2, rows, own] * v, 0, 1)

        @pl.when(s < STAGES - 1)
        def _():
            for p in range(PER):
                z_start(s + 1, c * PER + p)

    for c in range(PIECES):
        xs = pl.ds(pl.multiple_of(head(c), piece), piece)
        comb[0, xs, hz:hz + slab] = jnp.swapaxes(obs_ref[:, xs], 0, 1)
        if c == 0:
            pl.semaphore_wait(barrier, sum(there.astype(jnp.int32) for _, there in peers))
        z_start(0, c)

    for rev in (False, True):
        d = int(rev)
        hi, lo = split(toeplitz(place(kz_ref[...], 128, 1, 0, rev), slab)[:, :slab + 2 * hz])
        wz[d, :slab] = hi
        wz[d, slab:] = lo
        hi, lo = split(toeplitz(place(kx_ref[...], 8 * (part + 2 * hx), 8, 0, rev), part * 8))
        wx[d, :part * 8] = hi
        wx[d, part * 8:] = lo
        half = ky_ref.shape[1] // 2
        hi, lo = split(toeplitz(place(ky_ref[...], size_y + 256, 1, 128 - half, not rev), size_y)[:, 128:128 + size_y])
        wyh[d] = hi
        wyl[d] = lo

    def stage(s, _):
        zeros_z = jnp.zeros((1, hz, size_y), F32)
        zeros_x = jnp.zeros((1, slab, size_y), F32)

        def fill(there, ref, lo, n, zs, zeros):
            @pl.when(there)
            def _():
                def body(i, _):
                    ref[s, pl.ds(lo + i, 1), zs] = zeros
                    return 0
                lax.fori_loop(0, n, body, 0, unroll=4)

        fill(zg == 0, comb, 0, cols, pl.ds(0, hz), zeros_z)
        fill(zg == nz - 1, comb, 0, cols, pl.ds(hz + slab, hz), zeros_z)
        fill(gx == 0, g, 0, hx, pl.ds(0, slab), zeros_x)
        fill(gx == nx - 1, g, hx + cols, hx, pl.ds(0, slab), zeros_x)

        z_pass(s, 0)
        z_pass(s, 1)
        x_forward_on(s, 0)
        z_pass(s, 2)
        x_forward_on(s, 1)

        @pl.when(s > 0)
        def _():
            xy_pass(s - 1, CHUNKS - 1)

        z_pass(s, 3)
        z_pass(s, 4)
        xy_pass(s, 0)
        z_pass(s, 5)
        xy_pass(s, 1)
        z_pass(s, 6)
        z_pass(s, 7)
        xy_pass(s, 2)
        return 0

    lax.fori_loop(0, STAGES, stage, 0)
    xy_pass(STAGES - 1, CHUNKS - 1)

    def drain(s, _):
        for c in range(PIECES):
            z_sent(s, c)

        for p in range(PER):
            @pl.when(near_plain())
            def _():
                x_copy(s, 0, p).wait_send()

            @pl.when(x_seam)
            def _():
                x_copy(s, 0, p, X_DIRECT).wait_send()
                x_hop(s, p, 0).wait_send()

            @pl.when(x_forward)
            def _():
                x_hop(s, p, 1).wait_send()

            x_copy(s, 1, p).wait_send()
        return 0

    lax.fori_loop(0, STAGES, drain, 0)


def shards(nz, nx, observed, kernel_x, kernel_y, kernel_z):
    slab, cols, size_y = observed.shape
    part, piece = cols // CHUNKS, cols // PIECES
    wide = slab * 3
    out = pl.pallas_call(
        functools.partial(kernel, nz, nx),
        out_shape=jax.ShapeDtypeStruct((slab, cols, size_y), F32),
        in_specs=[pl.BlockSpec(memory_space=pltpu.VMEM)] * 4,
        out_specs=pl.BlockSpec(memory_space=pltpu.VMEM),
        scratch_shapes=[
            pltpu.VMEM((STAGES, cols, wide, size_y), F32),
            pltpu.VMEM((STAGES, cols + 2 * part, slab, size_y), F32),
            pltpu.VMEM((STAGES, PIECES, piece - Z_DIRECT, slab, size_y), F32),
            pltpu.VMEM((STAGES, PER, piece - X_DIRECT, slab, size_y), F32),
            pltpu.VMEM((2, 2 * slab, wide), BF),
            pltpu.VMEM((2, 16 * part, 24 * part), BF),
            pltpu.VMEM((2, size_y, size_y), BF),
            pltpu.VMEM((2, size_y, size_y), BF),
            pltpu.SemaphoreType.DMA((STAGES, PIECES, 2)),
            pltpu.SemaphoreType.DMA((STAGES, PIECES, 2)),
            pltpu.SemaphoreType.DMA((STAGES, 2, PER)),
            pltpu.SemaphoreType.DMA((STAGES, 2, PER)),
            pltpu.SemaphoreType.DMA((STAGES, PIECES)),
            pltpu.SemaphoreType.DMA((STAGES, PIECES)),
            pltpu.SemaphoreType.DMA((STAGES, PER)),
            pltpu.SemaphoreType.DMA((STAGES, PER)),
            pltpu.SemaphoreType.DMA((STAGES, PER)),
            pltpu.SemaphoreType.DMA((STAGES, PER)),
            pltpu.VMEM((part, slab, size_y), F32),
        ],
        compiler_params=pltpu.CompilerParams(
            collective_id=0, has_side_effects=True, vmem_limit_bytes=56 * 2**20
        ),
        name="deconvolve",
    )(
        observed,
        kernel_x.reshape(1, -1), kernel_y.reshape(1, -1), kernel_z.reshape(1, -1),
    )
    return out


def solution(mesh):
    return jax.shard_map(
        functools.partial(shards, mesh.shape["zg"], mesh.shape["gx"]),
        mesh=mesh,
        in_specs=(P("zg", "gx", None), P(), P(), P()),
        out_specs=P("zg", "gx", None),
        check_vma=False,
    )
```

```python
import functools

import jax
import jax.numpy as jnp
from jax import lax
from jax.experimental import pallas as pl
from jax.experimental.pallas import tpu as pltpu
from jax.sharding import PartitionSpec as P

STAGES = 4
CHUNKS = 4
PIECES = 8
PER = PIECES // CHUNKS
RING = 4
Z_DIRECT, X_DIRECT = 5, 4
X_ROUTES = ((4, 2), (6, 2))
MESH = pl.DeviceIdType.MESH
BF, F32 = jnp.bfloat16, jnp.float32


def split(v):
    hi = v.astype(BF)
    return hi, (v - hi.astype(F32)).astype(BF)


def mxu(a, b):
    return jnp.dot(a, b, preferred_element_type=F32)


def place(prof, width, step, start, rev):
    taps = prof.shape[1]
    h = prof / jnp.sum(prof)
    row = lax.broadcasted_iota(jnp.int32, (taps, width), 0)
    lane = lax.broadcasted_iota(jnp.int32, (taps, width), 1)
    t = (taps - 1 - row) if rev else row
    pick = jnp.where(lane == t * step + start, 1.0, 0.0).astype(F32)
    return lax.dot_general(
        jnp.broadcast_to(h, (8, taps)), pick, (((1,), (0,)), ((), ())),
        precision=lax.Precision.HIGHEST, preferred_element_type=F32,
    )[0:1]


def toeplitz(row, n):
    wide = jnp.broadcast_to(row, (n, row.shape[1]))
    return pltpu.roll(wide, 0, 1, stride=1, stride_axis=0)


def kernel(nz, nx, obs_ref, kx_ref, ky_ref, kz_ref, out_ref, comb, g, zfw, xfw, wz, wx, wyh, wyl,
           zsend, zrecv, xsend, xrecv, zbsend, zbrecv, xbsend, xbrecv, xfsend, xfrecv, xdone):
    slab, cols, size_y = out_ref.shape
    part, piece = cols // CHUNKS, cols // PIECES
    hz, hx = slab, part
    zg, gx = lax.axis_index("zg"), lax.axis_index("gx")
    odd = lax.rem(gx, 2)
    has_l, has_r = zg > 0, zg < nz - 1

    near = gx - 1 + 2 * odd
    far = gx + 1 - 2 * odd
    has_near = jnp.logical_and(gx > 0, gx < nx - 1)

    mid = nz // 2
    place_x = lax.rem(gx, RING)
    x_end = jnp.logical_or(place_x == 0, place_x == RING - 1)

    def corner(at):
        return zg == at

    seam_l, seam_r, first_z, last_z = corner(mid), corner(mid - 1), corner(0), corner(nz - 1)
    z_end, z_seam = jnp.logical_or(first_z, last_z), jnp.logical_or(seam_l, seam_r)
    turn = (1 - 2 * odd) * (RING - 1)
    over = RING * (1 - 2 * odd)
    skip = 2 * (1 - 2 * odd)
    x_seam = jnp.logical_and(x_end, has_near)
    x_forward = jnp.logical_and(x_end, jnp.logical_and(gx + over >= 0, gx + over < nx))
    x_from = jnp.logical_and(x_end, jnp.logical_and(gx - over >= 0, gx - over < nx))
    x_inner = jnp.logical_and(jnp.logical_not(x_end), jnp.logical_and(gx + skip >= 0, gx + skip < nx))
    x_ways = (x_forward, x_inner)

    barrier = pltpu.get_barrier_semaphore()
    peers = (
        ((zg - 1, gx), has_l), ((zg + 1, gx), has_r), ((zg, near), has_near), ((zg, far), gx >= 0),
        ((jnp.where(z_end, mid, 0), gx), jnp.logical_or(z_end, z_seam)),
        ((jnp.where(z_end, mid - 1, nz - 1), gx), jnp.logical_or(z_end, z_seam)),
        ((zg, gx + turn), x_end), ((zg, gx + over), x_forward), ((zg, gx - over), x_from),
        ((zg, gx + skip), x_inner), ((zg, gx - skip), x_from),
    )
    for peer, there in peers:
        @pl.when(there)
        def _():
            pl.semaphore_signal(barrier, inc=1, device_id=peer, device_id_type=MESH)

    def first(c):
        return part * (c + odd * (CHUNKS - 1 - 2 * c))

    def head(p):
        return piece * (p + odd * (PIECES - 1 - 2 * p))

    def z_copy(s, c, side, n=piece):
        rows = pl.ds(head(c), n)
        return pltpu.make_async_remote_copy(
            src_ref=comb.at[s, rows, pl.ds(hz, slab)],
            dst_ref=comb.at[s, rows, pl.ds((hz + slab) * (1 - side), slab)],
            send_sem=zsend.at[s, c, side], recv_sem=zrecv.at[s, c, side],
            device_id=(zg - 1 + 2 * side, gx), device_id_type=MESH,
        )

    def z_hop(s, c, side, hop):
        rows = pl.ds(head(c) + Z_DIRECT, piece - Z_DIRECT)
        if hop == 0:
            src, dst, to = comb.at[s, rows, pl.ds(hz, slab)], zfw.at[s, c], (nz - 1) * (1 - side)
        else:
            src, dst, to = zfw.at[s, c], comb.at[s, rows, pl.ds((hz + slab) * (1 - side), slab)], mid - 1 + side
        return pltpu.make_async_remote_copy(
            src_ref=src, dst_ref=dst, send_sem=zbsend.at[s, c], recv_sem=zbrecv.at[s, c],
            device_id=(to, gx), device_id_type=MESH,
        )

    z_sides = ((0, has_l, seam_l, last_z), (1, has_r, seam_r, first_z))

    def z_start(s, c):
        for side, there, seam, _ in z_sides:
            @pl.when(jnp.logical_and(there, jnp.logical_not(seam)))
            def _():
                z_copy(s, c, side).start()

            @pl.when(seam)
            def _():
                z_hop(s, c, side, 0).start()
                z_copy(s, c, side, Z_DIRECT).start()

    def z_sent(s, c):
        for side, there, seam, forwards in z_sides:
            @pl.when(jnp.logical_and(there, jnp.logical_not(seam)))
            def _():
                z_copy(s, c, side).wait_send()

            @pl.when(seam)
            def _():
                z_hop(s, c, side, 0).wait_send()
                z_copy(s, c, side, Z_DIRECT).wait_send()

            @pl.when(forwards)
            def _():
                z_hop(s, c, side, 1).wait_send()

    def z_arrived(s, c):
        for side, _, _, forwards in z_sides:
            @pl.when(forwards)
            def _():
                z_hop(s, c, side, 0).wait_recv()
                z_hop(s, c, side, 1).start()

        for side, there, seam in ((0, has_r, seam_r), (1, has_l, seam_l)):
            @pl.when(jnp.logical_and(there, jnp.logical_not(seam)))
            def _():
                z_copy(s, c, side).wait_recv()

            @pl.when(seam)
            def _():
                z_copy(s, c, side, Z_DIRECT).wait_recv()
                z_hop(s, c, side, 1).wait_recv()

    def x_hop(s, p, way, hop):
        lo, n = X_ROUTES[way]
        keep = xfw.at[s, p, pl.ds(lo - X_DIRECT, n)]
        if hop == 0:
            src, dst, to = g.at[s, pl.ds(hx + head(p) + lo, n)], keep, (far if way else gx + turn)
            sems = xbsend, xfrecv
        else:
            at = (1 - odd) * (hx - piece * (p + 1)) + odd * (hx + cols + piece * p)
            src, dst, to = keep, g.at[s, pl.ds(at + lo, n)], gx + (skip if way else over)
            sems = xfsend, xbrecv
        return pltpu.make_async_remote_copy(
            src_ref=src, dst_ref=dst, send_sem=sems[0].at[s, p, way], recv_sem=sems[1].at[s, p, way],
            device_id=(zg, to), device_id_type=MESH,
        )

    def x_copy(s, end, p, n=piece):
        at = head(p + end * (PIECES - PER))
        low = (odd + end) % 2
        to = at + (hx + cols) * (1 - low) - (cols - hx) * low
        return pltpu.make_async_remote_copy(
            src_ref=g.at[s, pl.ds(hx + at, n)],
            dst_ref=g.at[s, pl.ds(to, n)],
            send_sem=xsend.at[s, end, p], recv_sem=xrecv.at[s, end, p],
            device_id=(zg, near if end == 0 else far), device_id_type=MESH,
        )

    def near_plain():
        return jnp.logical_and(has_near, jnp.logical_not(x_seam))

    def x_forward_on(s, p):
        for way, there in enumerate(x_ways):
            @pl.when(there)
            def _():
                x_hop(s, p, way, 0).wait_recv()
                x_hop(s, p, way, 1).start()

    def z_pass(s, c):
        z_arrived(s, c)
        d = lax.rem(s, 2)
        both = wz[d]
        high = both[:slab]

        def column(i, _):
            hi, lo = split(comb[s, head(c) + i])
            top = mxu(both, hi)
            g[s, hx + head(c) + i] = top[:slab] + top[slab:] + mxu(high, lo)
            return 0

        lax.fori_loop(0, piece, column, 0, unroll=8)
        if c < PER:
            @pl.when(near_plain())
            def _():
                x_copy(s, 0, c).start()

            @pl.when(x_seam)
            def _():
                for way in range(2):
                    x_hop(s, c, way, 0).start()
                x_copy(s, 0, c, X_DIRECT).start()
        if c >= PIECES - PER:
            x_copy(s, 1, c - (PIECES - PER)).start()

    def xy_pass(s, c):
        if c == 0:
            for p in range(PER):
                @pl.when(near_plain())
                def _():
                    x_copy(s, 0, p).wait_recv()

                @pl.when(x_seam)
                def _():
                    x_copy(s, 0, p, X_DIRECT).wait_recv()
                    for way in range(2):
                        x_hop(s, p, way, 1).wait_recv()
        if c == CHUNKS - 1:
            for p in range(PER):
                x_copy(s, 1, p).wait_recv()
        d = lax.rem(s, 2)
        rows = pl.ds(first(c), part)
        n = part * 8

        def group(k, _):
            zs = pl.ds(pl.multiple_of(k * 8, 8), 8)
            hi, lo = split(g[s, pl.ds(first(c), part + 2 * hx), zs].reshape((part + 2 * hx) * 8, size_y))
            top = mxu(wx[d], hi)
            v = top[:n] + top[n:] + mxu(wx[d, :n], lo)
            xdone[:, zs] = v.reshape(part, 8, size_y)
            return 0

        lax.fori_loop(0, slab // 8, group, 0, unroll=4)
        hi, lo = split(xdone[...].reshape(part * slab, size_y))
        v = mxu(hi, wyh[d]) + mxu(lo, wyh[d]) + mxu(hi, wyl[d])
        v = v.reshape(part, slab, size_y)
        own = pl.ds(hz, slab)

        @pl.when(d == 0)
        def _():
            comb[s + 1, rows, own] = comb[0, rows, own] / v

        @pl.when(s == 1)
        def _():
            comb[2, rows, own] = comb[0, rows, own] * v

        @pl.when(s == STAGES - 1)
        def _():
            out_ref[:, pl.ds(pl.multiple_of(first(c), part), part)] = jnp.swapaxes(comb[2, rows, own] * v, 0, 1)

        late = CHUNKS - 2
        go = s < STAGES - 1
        if c == late:
            go = s < STAGES - 2

        @pl.when(go)
        def _():
            for p in range(PER):
                z_start(s + 1, c * PER + p)

        if c == CHUNKS - 1:
            @pl.when(s == STAGES - 2)
            def _():
                for p in range(PER):
                    z_start(s + 1, late * PER + p)

    for c in range(PIECES):
        xs = pl.ds(pl.multiple_of(head(c), piece), piece)
        comb[0, xs, hz:hz + slab] = jnp.swapaxes(obs_ref[:, xs], 0, 1)
        if c == 0:
            pl.semaphore_wait(barrier, sum(there.astype(jnp.int32) for _, there in peers))
        z_start(0, c)

    for rev in (False, True):
        d = int(rev)
        hi, lo = split(toeplitz(place(kz_ref[...], 128, 1, 0, rev), slab)[:, :slab + 2 * hz])
        wz[d, :slab] = hi
        wz[d, slab:] = lo
        hi, lo = split(toeplitz(place(kx_ref[...], 8 * (part + 2 * hx), 8, 0, rev), part * 8))
        wx[d, :part * 8] = hi
        wx[d, part * 8:] = lo
        half = ky_ref.shape[1] // 2
        hi, lo = split(toeplitz(place(ky_ref[...], size_y + 256, 1, 128 - half, not rev), size_y)[:, 128:128 + size_y])
        wyh[d] = hi
        wyl[d] = lo

    def begin(s):
        zeros_z = jnp.zeros((1, hz, size_y), F32)
        zeros_x = jnp.zeros((1, slab, size_y), F32)

        def fill(there, ref, lo, n, zs, zeros):
            @pl.when(there)
            def _():
                def body(i, _):
                    ref[s, pl.ds(lo + i, 1), zs] = zeros
                    return 0
                lax.fori_loop(0, n, body, 0, unroll=4)

        fill(zg == 0, comb, 0, cols, pl.ds(0, hz), zeros_z)
        fill(zg == nz - 1, comb, 0, cols, pl.ds(hz + slab, hz), zeros_z)
        fill(gx == 0, g, 0, hx, pl.ds(0, slab), zeros_x)
        fill(gx == nx - 1, g, hx + cols, hx, pl.ds(0, slab), zeros_x)

        z_pass(s, 0)
        z_pass(s, 1)
        x_forward_on(s, 0)
        z_pass(s, 2)
        x_forward_on(s, 1)

    def stage(s, _):
        begin(s)

        @pl.when(s > 0)
        def _():
            xy_pass(s - 1, 3)

        z_pass(s, 3)
        z_pass(s, 4)
        xy_pass(s, 0)
        z_pass(s, 5)
        xy_pass(s, 1)
        z_pass(s, 6)
        z_pass(s, 7)
        xy_pass(s, 2)
        return 0

    lax.fori_loop(0, STAGES - 1, stage, 0)
    s = STAGES - 1
    begin(s)
    xy_pass(s - 1, 3)
    z_pass(s, 3)
    z_pass(s, 6)
    z_pass(s, 7)
    xy_pass(s, 0)
    z_pass(s, 4)
    z_pass(s, 5)
    xy_pass(s, 1)
    xy_pass(s, 2)
    xy_pass(s, 3)

    def drain(s, _):
        for c in range(PIECES):
            z_sent(s, c)

        for p in range(PER):
            @pl.when(near_plain())
            def _():
                x_copy(s, 0, p).wait_send()

            @pl.when(x_seam)
            def _():
                x_copy(s, 0, p, X_DIRECT).wait_send()
                for way in range(2):
                    x_hop(s, p, way, 0).wait_send()

            for way, there in enumerate(x_ways):
                @pl.when(there)
                def _():
                    x_hop(s, p, way, 1).wait_send()

            x_copy(s, 1, p).wait_send()
        return 0

    lax.fori_loop(0, STAGES, drain, 0)


def shards(nz, nx, observed, kernel_x, kernel_y, kernel_z):
    slab, cols, size_y = observed.shape
    part, piece = cols // CHUNKS, cols // PIECES
    wide = slab * 3
    out = pl.pallas_call(
        functools.partial(kernel, nz, nx),
        out_shape=pltpu.VMEM((slab, cols, size_y), F32),
        in_specs=[pl.BlockSpec(memory_space=pltpu.VMEM)] * 4,
        out_specs=pl.BlockSpec(memory_space=pltpu.VMEM),
        scratch_shapes=[
            pltpu.VMEM((STAGES, cols, wide, size_y), F32),
            pltpu.VMEM((STAGES, cols + 2 * part, slab, size_y), F32),
            pltpu.VMEM((STAGES, PIECES, piece - Z_DIRECT, slab, size_y), F32),
            pltpu.VMEM((STAGES, PER, piece - X_DIRECT, slab, size_y), F32),
            pltpu.VMEM((2, 2 * slab, wide), BF),
            pltpu.VMEM((2, 16 * part, 24 * part), BF),
            pltpu.VMEM((2, size_y, size_y), BF),
            pltpu.VMEM((2, size_y, size_y), BF),
            pltpu.SemaphoreType.DMA((STAGES, PIECES, 2)),
            pltpu.SemaphoreType.DMA((STAGES, PIECES, 2)),
            pltpu.SemaphoreType.DMA((STAGES, 2, PER)),
            pltpu.SemaphoreType.DMA((STAGES, 2, PER)),
            pltpu.SemaphoreType.DMA((STAGES, PIECES)),
            pltpu.SemaphoreType.DMA((STAGES, PIECES)),
            pltpu.SemaphoreType.DMA((STAGES, PER, 2)),
            pltpu.SemaphoreType.DMA((STAGES, PER, 2)),
            pltpu.SemaphoreType.DMA((STAGES, PER, 2)),
            pltpu.SemaphoreType.DMA((STAGES, PER, 2)),
            pltpu.VMEM((part, slab, size_y), F32),
        ],
        compiler_params=pltpu.CompilerParams(
            collective_id=0, has_side_effects=True, vmem_limit_bytes=56 * 2**20
        ),
        name="deconvolve",
    )(
        observed,
        kernel_x.reshape(1, -1), kernel_y.reshape(1, -1), kernel_z.reshape(1, -1),
    )
    return pl.pallas_call(
        hand_over,
        out_shape=jax.ShapeDtypeStruct(out.shape, F32),
        in_specs=[pl.BlockSpec(memory_space=pltpu.VMEM)],
        out_specs=pl.BlockSpec(memory_space=pl.ANY),
        scratch_shapes=[pltpu.SemaphoreType.DMA((4,))],
        compiler_params=pltpu.CompilerParams(vmem_limit_bytes=8 * 2**20),
        name="hand_over",
    )(out)


def hand_over(src_ref, dst_ref, sem):
    n = src_ref.shape[0] // 4
    copies = [
        pltpu.make_async_copy(src_ref.at[pl.ds(k * n, n)], dst_ref.at[pl.ds(k * n, n)], sem.at[k])
        for k in range(4)
    ]
    for copy in copies:
        copy.start()
    for copy in copies:
        copy.wait()


def solution(mesh):
    return jax.shard_map(
        functools.partial(shards, mesh.shape["zg"], mesh.shape["gx"]),
        mesh=mesh,
        in_specs=(P("zg", "gx", None), P(), P(), P()),
        out_specs=P("zg", "gx", None),
        check_vma=False,
    )
```

```python
import functools

import jax
import jax.numpy as jnp
from jax import lax
from jax.experimental import pallas as pl
from jax.experimental.pallas import tpu as pltpu
from jax.sharding import PartitionSpec as P

STAGES = 4
CHUNKS = 4
PIECES = 8
PER = PIECES // CHUNKS
RING = 4
Z_DIRECT, X_DIRECT = 5, 3
X_ROUTES = ((3, 3), (6, 2))
MESH = pl.DeviceIdType.MESH
BF, F32 = jnp.bfloat16, jnp.float32


def split(v):
    hi = v.astype(BF)
    return hi, (v - hi.astype(F32)).astype(BF)


def mxu(a, b):
    return jnp.dot(a, b, preferred_element_type=F32)


def place(prof, width, step, start, rev):
    taps = prof.shape[1]
    h = prof / jnp.sum(prof)
    row = lax.broadcasted_iota(jnp.int32, (taps, width), 0)
    lane = lax.broadcasted_iota(jnp.int32, (taps, width), 1)
    t = (taps - 1 - row) if rev else row
    pick = jnp.where(lane == t * step + start, 1.0, 0.0).astype(F32)
    return lax.dot_general(
        jnp.broadcast_to(h, (8, taps)), pick, (((1,), (0,)), ((), ())),
        precision=lax.Precision.HIGHEST, preferred_element_type=F32,
    )[0:1]


def toeplitz(row, n):
    wide = jnp.broadcast_to(row, (n, row.shape[1]))
    return pltpu.roll(wide, 0, 1, stride=1, stride_axis=0)


def kernel(nz, nx, obs_ref, kx_ref, ky_ref, kz_ref, out_ref, comb, g, zfw, xfw, wz, wx, wx8, wyh, wyl,
           zsend, zrecv, xsend, xrecv, zbsend, zbrecv, xbsend, xbrecv, xfsend, xfrecv, xdone):
    slab, cols, size_y = out_ref.shape
    part, piece = cols // CHUNKS, cols // PIECES
    hz, hx = slab, part
    zg, gx = lax.axis_index("zg"), lax.axis_index("gx")
    odd = lax.rem(gx, 2)
    has_l, has_r = zg > 0, zg < nz - 1

    near = gx - 1 + 2 * odd
    far = gx + 1 - 2 * odd
    has_near = jnp.logical_and(gx > 0, gx < nx - 1)

    mid = nz // 2
    place_x = lax.rem(gx, RING)
    x_end = jnp.logical_or(place_x == 0, place_x == RING - 1)

    def corner(at):
        return zg == at

    seam_l, seam_r, first_z, last_z = corner(mid), corner(mid - 1), corner(0), corner(nz - 1)
    z_end, z_seam = jnp.logical_or(first_z, last_z), jnp.logical_or(seam_l, seam_r)
    turn = (1 - 2 * odd) * (RING - 1)
    over = RING * (1 - 2 * odd)
    skip = 2 * (1 - 2 * odd)
    x_seam = jnp.logical_and(x_end, has_near)
    x_forward = jnp.logical_and(x_end, jnp.logical_and(gx + over >= 0, gx + over < nx))
    x_from = jnp.logical_and(x_end, jnp.logical_and(gx - over >= 0, gx - over < nx))
    x_inner = jnp.logical_and(jnp.logical_not(x_end), jnp.logical_and(gx + skip >= 0, gx + skip < nx))
    x_ways = (x_forward, x_inner)

    barrier = pltpu.get_barrier_semaphore()
    peers = (
        ((zg - 1, gx), has_l), ((zg + 1, gx), has_r), ((zg, near), has_near), ((zg, far), gx >= 0),
        ((jnp.where(z_end, mid, 0), gx), jnp.logical_or(z_end, z_seam)),
        ((jnp.where(z_end, mid - 1, nz - 1), gx), jnp.logical_or(z_end, z_seam)),
        ((zg, gx + turn), x_end), ((zg, gx + over), x_forward), ((zg, gx - over), x_from),
        ((zg, gx + skip), x_inner), ((zg, gx - skip), x_from),
    )
    for peer, there in peers:
        @pl.when(there)
        def _():
            pl.semaphore_signal(barrier, inc=1, device_id=peer, device_id_type=MESH)

    def first(c):
        return part * (c + odd * (CHUNKS - 1 - 2 * c))

    def head(p):
        return piece * (p + odd * (PIECES - 1 - 2 * p))

    def z_copy(s, c, side, n=piece):
        rows = pl.ds(head(c), n)
        return pltpu.make_async_remote_copy(
            src_ref=comb.at[s, rows, pl.ds(hz, slab)],
            dst_ref=comb.at[s, rows, pl.ds((hz + slab) * (1 - side), slab)],
            send_sem=zsend.at[s, c, side], recv_sem=zrecv.at[s, c, side],
            device_id=(zg - 1 + 2 * side, gx), device_id_type=MESH,
        )

    def z_hop(s, c, side, hop):
        rows = pl.ds(head(c) + Z_DIRECT, piece - Z_DIRECT)
        if hop == 0:
            src, dst, to = comb.at[s, rows, pl.ds(hz, slab)], zfw.at[s, c], (nz - 1) * (1 - side)
        else:
            src, dst, to = zfw.at[s, c], comb.at[s, rows, pl.ds((hz + slab) * (1 - side), slab)], mid - 1 + side
        return pltpu.make_async_remote_copy(
            src_ref=src, dst_ref=dst, send_sem=zbsend.at[s, c], recv_sem=zbrecv.at[s, c],
            device_id=(to, gx), device_id_type=MESH,
        )

    z_sides = ((0, has_l, seam_l, last_z), (1, has_r, seam_r, first_z))

    def z_start(s, c):
        for side, there, seam, _ in z_sides:
            @pl.when(jnp.logical_and(there, jnp.logical_not(seam)))
            def _():
                z_copy(s, c, side).start()

            @pl.when(seam)
            def _():
                z_hop(s, c, side, 0).start()
                z_copy(s, c, side, Z_DIRECT).start()

    def z_sent(s, c):
        for side, there, seam, forwards in z_sides:
            @pl.when(jnp.logical_and(there, jnp.logical_not(seam)))
            def _():
                z_copy(s, c, side).wait_send()

            @pl.when(seam)
            def _():
                z_hop(s, c, side, 0).wait_send()
                z_copy(s, c, side, Z_DIRECT).wait_send()

            @pl.when(forwards)
            def _():
                z_hop(s, c, side, 1).wait_send()

    def z_arrived(s, c):
        for side, _, _, forwards in z_sides:
            @pl.when(forwards)
            def _():
                z_hop(s, c, side, 0).wait_recv()
                z_hop(s, c, side, 1).start()

        for side, there, seam in ((0, has_r, seam_r), (1, has_l, seam_l)):
            @pl.when(jnp.logical_and(there, jnp.logical_not(seam)))
            def _():
                z_copy(s, c, side).wait_recv()

            @pl.when(seam)
            def _():
                z_copy(s, c, side, Z_DIRECT).wait_recv()
                z_hop(s, c, side, 1).wait_recv()

    def x_hop(s, p, way, hop):
        lo, n = X_ROUTES[way]
        keep = xfw.at[s, p, pl.ds(lo - X_DIRECT, n)]
        if hop == 0:
            src, dst, to = g.at[s, pl.ds(hx + head(p) + lo, n)], keep, (far if way else gx + turn)
            sems = xbsend, xfrecv
        else:
            at = (1 - odd) * (hx - piece * (p + 1)) + odd * (hx + cols + piece * p)
            src, dst, to = keep, g.at[s, pl.ds(at + lo, n)], gx + (skip if way else over)
            sems = xfsend, xbrecv
        return pltpu.make_async_remote_copy(
            src_ref=src, dst_ref=dst, send_sem=sems[0].at[s, p, way], recv_sem=sems[1].at[s, p, way],
            device_id=(zg, to), device_id_type=MESH,
        )

    def x_copy(s, end, p, n=piece):
        at = head(p + end * (PIECES - PER))
        low = (odd + end) % 2
        to = at + (hx + cols) * (1 - low) - (cols - hx) * low
        return pltpu.make_async_remote_copy(
            src_ref=g.at[s, pl.ds(hx + at, n)],
            dst_ref=g.at[s, pl.ds(to, n)],
            send_sem=xsend.at[s, end, p], recv_sem=xrecv.at[s, end, p],
            device_id=(zg, near if end == 0 else far), device_id_type=MESH,
        )

    def near_plain():
        return jnp.logical_and(has_near, jnp.logical_not(x_seam))

    def x_forward_on(s, p):
        for way, there in enumerate(x_ways):
            @pl.when(there)
            def _():
                x_hop(s, p, way, 0).wait_recv()
                x_hop(s, p, way, 1).start()

    def z_pass(s, c):
        z_arrived(s, c)
        d = lax.rem(s, 2)
        both = wz[d]
        high = both[:slab]

        def column(i, _):
            hi, lo = split(comb[s, head(c) + i])
            top = mxu(both, hi)
            g[s, hx + head(c) + i] = top[:slab] + top[slab:] + mxu(high, lo)
            return 0

        lax.fori_loop(0, piece, column, 0, unroll=8)
        if c < PER:
            @pl.when(near_plain())
            def _():
                x_copy(s, 0, c).start()

            @pl.when(x_seam)
            def _():
                for way in range(2):
                    x_hop(s, c, way, 0).start()
                x_copy(s, 0, c, X_DIRECT).start()
        if c >= PIECES - PER:
            x_copy(s, 1, c - (PIECES - PER)).start()

    def near_arrived(s, p):
        @pl.when(near_plain())
        def _():
            x_copy(s, 0, p).wait_recv()

        @pl.when(x_seam)
        def _():
            x_copy(s, 0, p, X_DIRECT).wait_recv()
            for way in range(2):
                x_hop(s, p, way, 1).wait_recv()

    def lateral(s, at, width, band):
        d = lax.rem(s, 2)
        rows = pl.ds(at, width)
        n = width * 8

        def group(k, _):
            zs = pl.ds(pl.multiple_of(k * 8, 8), 8)
            hi, lo = split(g[s, pl.ds(at, width + 2 * hx), zs].reshape((width + 2 * hx) * 8, size_y))
            top = mxu(band[d], hi)
            v = top[:n] + top[n:] + mxu(band[d, :n], lo)
            xdone[:width, zs] = v.reshape(width, 8, size_y)
            return 0

        lax.fori_loop(0, slab // 8, group, 0, unroll=4)
        hi, lo = split(xdone[:width].reshape(width * slab, size_y))
        v = mxu(hi, wyh[d]) + mxu(lo, wyh[d]) + mxu(hi, wyl[d])
        v = v.reshape(width, slab, size_y)
        own = pl.ds(hz, slab)

        @pl.when(d == 0)
        def _():
            comb[s + 1, rows, own] = comb[0, rows, own] / v

        @pl.when(s == 1)
        def _():
            comb[2, rows, own] = comb[0, rows, own] * v

        @pl.when(s == STAGES - 1)
        def _():
            out_ref[:, pl.ds(pl.multiple_of(at, width), width)] = jnp.swapaxes(comb[2, rows, own] * v, 0, 1)

    def send_on(s, c):
        late = CHUNKS - 2

        @pl.when(s < STAGES - (2 if c == late else 1))
        def _():
            for p in range(PER):
                z_start(s + 1, c * PER + p)

        if c == CHUNKS - 1:
            @pl.when(s == STAGES - 2)
            def _():
                for p in range(PER):
                    z_start(s + 1, late * PER + p)

    def xy_pass(s, c):
        if c == CHUNKS - 1:
            for p in range(PER):
                x_copy(s, 1, p).wait_recv()
        lateral(s, first(c), part, wx)
        send_on(s, c)

    def near_inner(s):
        near_arrived(s, 0)
        lateral(s, head(1), piece, wx8)

    def near_edge(s):
        near_arrived(s, 1)
        lateral(s, head(0), piece, wx8)
        send_on(s, 0)

    for c in range(PIECES):
        xs = pl.ds(pl.multiple_of(head(c), piece), piece)
        comb[0, xs, hz:hz + slab] = jnp.swapaxes(obs_ref[:, xs], 0, 1)
        if c == 0:
            pl.semaphore_wait(barrier, sum(there.astype(jnp.int32) for _, there in peers))
        z_start(0, c)

    for rev in (False, True):
        d = int(rev)
        hi, lo = split(toeplitz(place(kz_ref[...], 128, 1, 0, rev), slab)[:, :slab + 2 * hz])
        wz[d, :slab] = hi
        wz[d, slab:] = lo
        hi, lo = split(toeplitz(place(kx_ref[...], 8 * (part + 2 * hx), 8, 0, rev), part * 8))
        wx[d, :part * 8] = hi
        wx[d, part * 8:] = lo
        n, k = piece * 8, 8 * (piece + 2 * hx)
        wx8[d, :n] = hi[:n, :k]
        wx8[d, n:] = lo[:n, :k]
        half = ky_ref.shape[1] // 2
        hi, lo = split(toeplitz(place(ky_ref[...], size_y + 256, 1, 128 - half, not rev), size_y)[:, 128:128 + size_y])
        wyh[d] = hi
        wyl[d] = lo

    def begin(s):
        zeros_z = jnp.zeros((1, hz, size_y), F32)
        zeros_x = jnp.zeros((1, slab, size_y), F32)

        def fill(there, ref, lo, n, zs, zeros):
            @pl.when(there)
            def _():
                def body(i, _):
                    ref[s, pl.ds(lo + i, 1), zs] = zeros
                    return 0
                lax.fori_loop(0, n, body, 0, unroll=4)

        fill(zg == 0, comb, 0, cols, pl.ds(0, hz), zeros_z)
        fill(zg == nz - 1, comb, 0, cols, pl.ds(hz + slab, hz), zeros_z)
        fill(gx == 0, g, 0, hx, pl.ds(0, slab), zeros_x)
        fill(gx == nx - 1, g, hx + cols, hx, pl.ds(0, slab), zeros_x)

        z_pass(s, 0)
        z_pass(s, 1)
        x_forward_on(s, 0)
        z_pass(s, 2)
        x_forward_on(s, 1)

    def stage(s, _):
        begin(s)

        @pl.when(s > 0)
        def _():
            xy_pass(s - 1, 3)

        z_pass(s, 3)
        near_inner(s)
        z_pass(s, 4)
        near_edge(s)
        z_pass(s, 5)
        xy_pass(s, 1)
        z_pass(s, 6)
        z_pass(s, 7)
        xy_pass(s, 2)
        return 0

    lax.fori_loop(0, STAGES - 1, stage, 0)
    s = STAGES - 1
    begin(s)
    xy_pass(s - 1, 3)
    z_pass(s, 3)
    z_pass(s, 6)
    z_pass(s, 7)
    near_inner(s)
    near_edge(s)
    z_pass(s, 4)
    z_pass(s, 5)
    xy_pass(s, 1)
    xy_pass(s, 2)
    xy_pass(s, 3)

    def drain(s, _):
        for c in range(PIECES):
            z_sent(s, c)

        for p in range(PER):
            @pl.when(near_plain())
            def _():
                x_copy(s, 0, p).wait_send()

            @pl.when(x_seam)
            def _():
                x_copy(s, 0, p, X_DIRECT).wait_send()
                for way in range(2):
                    x_hop(s, p, way, 0).wait_send()

            for way, there in enumerate(x_ways):
                @pl.when(there)
                def _():
                    x_hop(s, p, way, 1).wait_send()

            x_copy(s, 1, p).wait_send()
        return 0

    lax.fori_loop(0, STAGES, drain, 0)


def shards(nz, nx, observed, kernel_x, kernel_y, kernel_z):
    slab, cols, size_y = observed.shape
    part, piece = cols // CHUNKS, cols // PIECES
    wide = slab * 3
    out = pl.pallas_call(
        functools.partial(kernel, nz, nx),
        out_shape=pltpu.VMEM((slab, cols, size_y), F32),
        in_specs=[pl.BlockSpec(memory_space=pltpu.VMEM)] * 4,
        out_specs=pl.BlockSpec(memory_space=pltpu.VMEM),
        scratch_shapes=[
            pltpu.VMEM((STAGES, cols, wide, size_y), F32),
            pltpu.VMEM((STAGES, cols + 2 * part, slab, size_y), F32),
            pltpu.VMEM((STAGES, PIECES, piece - Z_DIRECT, slab, size_y), F32),
            pltpu.VMEM((STAGES, PER, piece - X_DIRECT, slab, size_y), F32),
            pltpu.VMEM((2, 2 * slab, wide), BF),
            pltpu.VMEM((2, 16 * part, 24 * part), BF),
            pltpu.VMEM((2, 16 * piece, 8 * (piece + 2 * part)), BF),
            pltpu.VMEM((2, size_y, size_y), BF),
            pltpu.VMEM((2, size_y, size_y), BF),
            pltpu.SemaphoreType.DMA((STAGES, PIECES, 2)),
            pltpu.SemaphoreType.DMA((STAGES, PIECES, 2)),
            pltpu.SemaphoreType.DMA((STAGES, 2, PER)),
            pltpu.SemaphoreType.DMA((STAGES, 2, PER)),
            pltpu.SemaphoreType.DMA((STAGES, PIECES)),
            pltpu.SemaphoreType.DMA((STAGES, PIECES)),
            pltpu.SemaphoreType.DMA((STAGES, PER, 2)),
            pltpu.SemaphoreType.DMA((STAGES, PER, 2)),
            pltpu.SemaphoreType.DMA((STAGES, PER, 2)),
            pltpu.SemaphoreType.DMA((STAGES, PER, 2)),
            pltpu.VMEM((part, slab, size_y), F32),
        ],
        compiler_params=pltpu.CompilerParams(
            collective_id=0, has_side_effects=True, vmem_limit_bytes=56 * 2**20
        ),
        name="deconvolve",
    )(
        observed,
        kernel_x.reshape(1, -1), kernel_y.reshape(1, -1), kernel_z.reshape(1, -1),
    )
    return pl.pallas_call(
        hand_over,
        out_shape=jax.ShapeDtypeStruct(out.shape, F32),
        in_specs=[pl.BlockSpec(memory_space=pltpu.VMEM)],
        out_specs=pl.BlockSpec(memory_space=pl.ANY),
        scratch_shapes=[pltpu.SemaphoreType.DMA((4,))],
        compiler_params=pltpu.CompilerParams(vmem_limit_bytes=8 * 2**20),
        name="hand_over",
    )(out)


def hand_over(src_ref, dst_ref, sem):
    n = src_ref.shape[0] // 4
    copies = [
        pltpu.make_async_copy(src_ref.at[pl.ds(k * n, n)], dst_ref.at[pl.ds(k * n, n)], sem.at[k])
        for k in range(4)
    ]
    for copy in copies:
        copy.start()
    for copy in copies:
        copy.wait()


def solution(mesh):
    return jax.shard_map(
        functools.partial(shards, mesh.shape["zg"], mesh.shape["gx"]),
        mesh=mesh,
        in_specs=(P("zg", "gx", None), P(), P(), P()),
        out_specs=P("zg", "gx", None),
        check_vma=False,
    )
```

```python
import functools

import jax
import jax.numpy as jnp
from jax import lax
from jax.experimental import pallas as pl
from jax.experimental.pallas import tpu as pltpu
from jax.sharding import PartitionSpec as P

STAGES = 4
CHUNKS = 4
PIECES = 8
PER = PIECES // CHUNKS
RING = 4
Z_DIRECT, X_DIRECT = 5, 3
X_ROUTES = ((3, 3), (6, 2))
MESH = pl.DeviceIdType.MESH
BF, F32 = jnp.bfloat16, jnp.float32


def split(v):
    hi = v.astype(BF)
    return hi, (v - hi.astype(F32)).astype(BF)


def mxu(a, b):
    return jnp.dot(a, b, preferred_element_type=F32)


def place(prof, width, step, start, rev):
    taps = prof.shape[1]
    h = prof / jnp.sum(prof)
    row = lax.broadcasted_iota(jnp.int32, (taps, width), 0)
    lane = lax.broadcasted_iota(jnp.int32, (taps, width), 1)
    t = (taps - 1 - row) if rev else row
    pick = jnp.where(lane == t * step + start, 1.0, 0.0).astype(F32)
    return lax.dot_general(
        jnp.broadcast_to(h, (8, taps)), pick, (((1,), (0,)), ((), ())),
        precision=lax.Precision.HIGHEST, preferred_element_type=F32,
    )[0:1]


def toeplitz(row, n):
    wide = jnp.broadcast_to(row, (n, row.shape[1]))
    return pltpu.roll(wide, 0, 1, stride=1, stride_axis=0)


def kernel(nz, nx, obs_ref, kx_ref, ky_ref, kz_ref, out_ref, comb, g, zfw, xfw, wz, wx, wx8, wyh, wyl,
           zsend, zrecv, xsend, xrecv, zbsend, zbrecv, xbsend, xbrecv, xfsend, xfrecv, xdone, loaded, loadsem):
    slab, cols, size_y = out_ref.shape
    part, piece = cols // CHUNKS, cols // PIECES
    hz, hx = slab, part
    zg, gx = lax.axis_index("zg"), lax.axis_index("gx")
    odd = lax.rem(gx, 2)
    has_l, has_r = zg > 0, zg < nz - 1

    near = gx - 1 + 2 * odd
    far = gx + 1 - 2 * odd
    has_near = jnp.logical_and(gx > 0, gx < nx - 1)

    mid = nz // 2
    place_x = lax.rem(gx, RING)
    x_end = jnp.logical_or(place_x == 0, place_x == RING - 1)

    def corner(at):
        return zg == at

    seam_l, seam_r, first_z, last_z = corner(mid), corner(mid - 1), corner(0), corner(nz - 1)
    z_end, z_seam = jnp.logical_or(first_z, last_z), jnp.logical_or(seam_l, seam_r)
    turn = (1 - 2 * odd) * (RING - 1)
    over = RING * (1 - 2 * odd)
    skip = 2 * (1 - 2 * odd)
    x_seam = jnp.logical_and(x_end, has_near)
    x_forward = jnp.logical_and(x_end, jnp.logical_and(gx + over >= 0, gx + over < nx))
    x_from = jnp.logical_and(x_end, jnp.logical_and(gx - over >= 0, gx - over < nx))
    x_inner = jnp.logical_and(jnp.logical_not(x_end), jnp.logical_and(gx + skip >= 0, gx + skip < nx))
    x_ways = (x_forward, x_inner)

    def head(p):
        return piece * (p + odd * (PIECES - 1 - 2 * p))

    def load(c):
        xs = pl.ds(pl.multiple_of(head(c), piece), piece)
        return pltpu.make_async_copy(obs_ref.at[:, xs], loaded.at[:, xs], loadsem.at[c])

    for c in range(PIECES):
        load(c).start()

    barrier = pltpu.get_barrier_semaphore()
    peers = (
        ((zg - 1, gx), has_l), ((zg + 1, gx), has_r), ((zg, near), has_near), ((zg, far), gx >= 0),
        ((jnp.where(z_end, mid, 0), gx), jnp.logical_or(z_end, z_seam)),
        ((jnp.where(z_end, mid - 1, nz - 1), gx), jnp.logical_or(z_end, z_seam)),
        ((zg, gx + turn), x_end), ((zg, gx + over), x_forward), ((zg, gx - over), x_from),
        ((zg, gx + skip), x_inner), ((zg, gx - skip), x_from),
    )
    for peer, there in peers:
        @pl.when(there)
        def _():
            pl.semaphore_signal(barrier, inc=1, device_id=peer, device_id_type=MESH)

    def first(c):
        return part * (c + odd * (CHUNKS - 1 - 2 * c))

    def z_copy(s, c, side, n=piece):
        rows = pl.ds(head(c), n)
        return pltpu.make_async_remote_copy(
            src_ref=comb.at[s, rows, pl.ds(hz, slab)],
            dst_ref=comb.at[s, rows, pl.ds((hz + slab) * (1 - side), slab)],
            send_sem=zsend.at[s, c, side], recv_sem=zrecv.at[s, c, side],
            device_id=(zg - 1 + 2 * side, gx), device_id_type=MESH,
        )

    def z_hop(s, c, side, hop):
        rows = pl.ds(head(c) + Z_DIRECT, piece - Z_DIRECT)
        if hop == 0:
            src, dst, to = comb.at[s, rows, pl.ds(hz, slab)], zfw.at[s, c], (nz - 1) * (1 - side)
        else:
            src, dst, to = zfw.at[s, c], comb.at[s, rows, pl.ds((hz + slab) * (1 - side), slab)], mid - 1 + side
        return pltpu.make_async_remote_copy(
            src_ref=src, dst_ref=dst, send_sem=zbsend.at[s, c], recv_sem=zbrecv.at[s, c],
            device_id=(to, gx), device_id_type=MESH,
        )

    z_sides = ((0, has_l, seam_l, last_z), (1, has_r, seam_r, first_z))

    def z_start(s, c):
        for side, there, seam, _ in z_sides:
            @pl.when(jnp.logical_and(there, jnp.logical_not(seam)))
            def _():
                z_copy(s, c, side).start()

            @pl.when(seam)
            def _():
                z_hop(s, c, side, 0).start()
                z_copy(s, c, side, Z_DIRECT).start()

    def z_sent(s, c):
        for side, there, seam, forwards in z_sides:
            @pl.when(jnp.logical_and(there, jnp.logical_not(seam)))
            def _():
                z_copy(s, c, side).wait_send()

            @pl.when(seam)
            def _():
                z_hop(s, c, side, 0).wait_send()
                z_copy(s, c, side, Z_DIRECT).wait_send()

            @pl.when(forwards)
            def _():
                z_hop(s, c, side, 1).wait_send()

    def z_arrived(s, c):
        for side, _, _, forwards in z_sides:
            @pl.when(forwards)
            def _():
                z_hop(s, c, side, 0).wait_recv()
                z_hop(s, c, side, 1).start()

        for side, there, seam in ((0, has_r, seam_r), (1, has_l, seam_l)):
            @pl.when(jnp.logical_and(there, jnp.logical_not(seam)))
            def _():
                z_copy(s, c, side).wait_recv()

            @pl.when(seam)
            def _():
                z_copy(s, c, side, Z_DIRECT).wait_recv()
                z_hop(s, c, side, 1).wait_recv()

    def x_hop(s, p, way, hop):
        lo, n = X_ROUTES[way]
        keep = xfw.at[s, p, pl.ds(lo - X_DIRECT, n)]
        if hop == 0:
            src, dst, to = g.at[s, pl.ds(hx + head(p) + lo, n)], keep, (far if way else gx + turn)
            sems = xbsend, xfrecv
        else:
            at = (1 - odd) * (hx - piece * (p + 1)) + odd * (hx + cols + piece * p)
            src, dst, to = keep, g.at[s, pl.ds(at + lo, n)], gx + (skip if way else over)
            sems = xfsend, xbrecv
        return pltpu.make_async_remote_copy(
            src_ref=src, dst_ref=dst, send_sem=sems[0].at[s, p, way], recv_sem=sems[1].at[s, p, way],
            device_id=(zg, to), device_id_type=MESH,
        )

    def x_copy(s, end, p, n=piece):
        at = head(p + end * (PIECES - PER))
        low = (odd + end) % 2
        to = at + (hx + cols) * (1 - low) - (cols - hx) * low
        return pltpu.make_async_remote_copy(
            src_ref=g.at[s, pl.ds(hx + at, n)],
            dst_ref=g.at[s, pl.ds(to, n)],
            send_sem=xsend.at[s, end, p], recv_sem=xrecv.at[s, end, p],
            device_id=(zg, near if end == 0 else far), device_id_type=MESH,
        )

    def near_plain():
        return jnp.logical_and(has_near, jnp.logical_not(x_seam))

    def x_forward_on(s, p):
        for way, there in enumerate(x_ways):
            @pl.when(there)
            def _():
                x_hop(s, p, way, 0).wait_recv()
                x_hop(s, p, way, 1).start()

    def z_pass(s, c):
        z_arrived(s, c)
        d = lax.rem(s, 2)
        both = wz[d]
        high = both[:slab]

        def column(i, _):
            hi, lo = split(comb[s, head(c) + i])
            top = mxu(both, hi)
            g[s, hx + head(c) + i] = top[:slab] + top[slab:] + mxu(high, lo)
            return 0

        lax.fori_loop(0, piece, column, 0, unroll=8)
        if c < PER:
            @pl.when(near_plain())
            def _():
                x_copy(s, 0, c).start()

            @pl.when(x_seam)
            def _():
                for way in range(2):
                    x_hop(s, c, way, 0).start()
                x_copy(s, 0, c, X_DIRECT).start()
        if c >= PIECES - PER:
            x_copy(s, 1, c - (PIECES - PER)).start()

    def near_arrived(s, p):
        @pl.when(near_plain())
        def _():
            x_copy(s, 0, p).wait_recv()

        @pl.when(x_seam)
        def _():
            x_copy(s, 0, p, X_DIRECT).wait_recv()
            for way in range(2):
                x_hop(s, p, way, 1).wait_recv()

    def lateral(s, at, width, band):
        d = lax.rem(s, 2)
        rows = pl.ds(at, width)
        n = width * 8

        def group(k, _):
            zs = pl.ds(pl.multiple_of(k * 8, 8), 8)
            hi, lo = split(g[s, pl.ds(at, width + 2 * hx), zs].reshape((width + 2 * hx) * 8, size_y))
            top = mxu(band[d], hi)
            v = top[:n] + top[n:] + mxu(band[d, :n], lo)
            xdone[:width, zs] = v.reshape(width, 8, size_y)
            return 0

        lax.fori_loop(0, slab // 8, group, 0, unroll=4)
        hi, lo = split(xdone[:width].reshape(width * slab, size_y))
        v = mxu(hi, wyh[d]) + mxu(lo, wyh[d]) + mxu(hi, wyl[d])
        v = v.reshape(width, slab, size_y)
        own = pl.ds(hz, slab)

        @pl.when(d == 0)
        def _():
            comb[s + 1, rows, own] = comb[0, rows, own] / v

        @pl.when(s == 1)
        def _():
            comb[2, rows, own] = comb[0, rows, own] * v

        @pl.when(s == STAGES - 1)
        def _():
            out_ref[:, pl.ds(pl.multiple_of(at, width), width)] = jnp.swapaxes(comb[2, rows, own] * v, 0, 1)

    def send_on(s, c):
        late = CHUNKS - 2

        @pl.when(s < STAGES - (2 if c == late else 1))
        def _():
            for p in range(PER):
                z_start(s + 1, c * PER + p)

        if c == CHUNKS - 1:
            @pl.when(s == STAGES - 2)
            def _():
                for p in range(PER):
                    z_start(s + 1, late * PER + p)

    def xy_pass(s, c):
        if c == CHUNKS - 1:
            for p in range(PER):
                x_copy(s, 1, p).wait_recv()
        lateral(s, first(c), part, wx)
        send_on(s, c)

    def near_inner(s):
        near_arrived(s, 0)
        lateral(s, head(1), piece, wx8)

    def near_edge(s):
        near_arrived(s, 1)
        lateral(s, head(0), piece, wx8)
        send_on(s, 0)

    for c in range(PIECES):
        xs = pl.ds(pl.multiple_of(head(c), piece), piece)
        load(c).wait()
        comb[0, xs, hz:hz + slab] = jnp.swapaxes(loaded[:, xs], 0, 1)
        if c == 0:
            pl.semaphore_wait(barrier, sum(there.astype(jnp.int32) for _, there in peers))
        z_start(0, c)

    for rev in (False, True):
        d = int(rev)
        hi, lo = split(toeplitz(place(kz_ref[...], 128, 1, 0, rev), slab)[:, :slab + 2 * hz])
        wz[d, :slab] = hi
        wz[d, slab:] = lo
        hi, lo = split(toeplitz(place(kx_ref[...], 8 * (part + 2 * hx), 8, 0, rev), part * 8))
        wx[d, :part * 8] = hi
        wx[d, part * 8:] = lo
        n, k = piece * 8, 8 * (piece + 2 * hx)
        wx8[d, :n] = hi[:n, :k]
        wx8[d, n:] = lo[:n, :k]
        half = ky_ref.shape[1] // 2
        hi, lo = split(toeplitz(place(ky_ref[...], size_y + 256, 1, 128 - half, not rev), size_y)[:, 128:128 + size_y])
        wyh[d] = hi
        wyl[d] = lo

    def clear(s):
        zeros_z = jnp.zeros((1, hz, size_y), F32)
        zeros_x = jnp.zeros((1, slab, size_y), F32)

        def fill(there, ref, lo, n, zs, zeros):
            @pl.when(there)
            def _():
                def body(i, _):
                    ref[s, pl.ds(lo + i, 1), zs] = zeros
                    return 0
                lax.fori_loop(0, n, body, 0, unroll=4)

        fill(zg == 0, comb, 0, cols, pl.ds(0, hz), zeros_z)
        fill(zg == nz - 1, comb, 0, cols, pl.ds(hz + slab, hz), zeros_z)
        fill(gx == 0, g, 0, hx, pl.ds(0, slab), zeros_x)
        fill(gx == nx - 1, g, hx + cols, hx, pl.ds(0, slab), zeros_x)

    def begin(s):
        z_pass(s, 0)
        z_pass(s, 1)
        x_forward_on(s, 0)
        z_pass(s, 2)
        x_forward_on(s, 1)

    def stage(s, _):
        begin(s)

        @pl.when(s > 0)
        def _():
            xy_pass(s - 1, 3)

        z_pass(s, 3)
        z_pass(s, 4)
        near_inner(s)
        z_pass(s, 5)
        near_edge(s)
        xy_pass(s, 1)
        z_pass(s, 6)
        z_pass(s, 7)
        xy_pass(s, 2)
        clear(s + 1)
        return 0

    clear(0)
    lax.fori_loop(0, STAGES - 1, stage, 0)
    s = STAGES - 1
    begin(s)
    xy_pass(s - 1, 3)
    z_pass(s, 3)
    z_pass(s, 6)
    z_pass(s, 7)
    near_inner(s)
    near_edge(s)
    z_pass(s, 4)
    z_pass(s, 5)
    xy_pass(s, 1)
    xy_pass(s, 2)
    xy_pass(s, 3)

    def drain(s, _):
        for c in range(PIECES):
            z_sent(s, c)

        for p in range(PER):
            @pl.when(near_plain())
            def _():
                x_copy(s, 0, p).wait_send()

            @pl.when(x_seam)
            def _():
                x_copy(s, 0, p, X_DIRECT).wait_send()
                for way in range(2):
                    x_hop(s, p, way, 0).wait_send()

            for way, there in enumerate(x_ways):
                @pl.when(there)
                def _():
                    x_hop(s, p, way, 1).wait_send()

            x_copy(s, 1, p).wait_send()
        return 0

    lax.fori_loop(0, STAGES, drain, 0)


def shards(nz, nx, observed, kernel_x, kernel_y, kernel_z):
    slab, cols, size_y = observed.shape
    part, piece = cols // CHUNKS, cols // PIECES
    wide = slab * 3
    out = pl.pallas_call(
        functools.partial(kernel, nz, nx),
        out_shape=pltpu.VMEM((slab, cols, size_y), F32),
        in_specs=[pl.BlockSpec(memory_space=pltpu.HBM)] + [pl.BlockSpec(memory_space=pltpu.VMEM)] * 3,
        out_specs=pl.BlockSpec(memory_space=pltpu.VMEM),
        scratch_shapes=[
            pltpu.VMEM((STAGES, cols, wide, size_y), F32),
            pltpu.VMEM((STAGES, cols + 2 * part, slab, size_y), F32),
            pltpu.VMEM((STAGES, PIECES, piece - Z_DIRECT, slab, size_y), F32),
            pltpu.VMEM((STAGES, PER, piece - X_DIRECT, slab, size_y), F32),
            pltpu.VMEM((2, 2 * slab, wide), BF),
            pltpu.VMEM((2, 16 * part, 24 * part), BF),
            pltpu.VMEM((2, 16 * piece, 8 * (piece + 2 * part)), BF),
            pltpu.VMEM((2, size_y, size_y), BF),
            pltpu.VMEM((2, size_y, size_y), BF),
            pltpu.SemaphoreType.DMA((STAGES, PIECES, 2)),
            pltpu.SemaphoreType.DMA((STAGES, PIECES, 2)),
            pltpu.SemaphoreType.DMA((STAGES, 2, PER)),
            pltpu.SemaphoreType.DMA((STAGES, 2, PER)),
            pltpu.SemaphoreType.DMA((STAGES, PIECES)),
            pltpu.SemaphoreType.DMA((STAGES, PIECES)),
            pltpu.SemaphoreType.DMA((STAGES, PER, 2)),
            pltpu.SemaphoreType.DMA((STAGES, PER, 2)),
            pltpu.SemaphoreType.DMA((STAGES, PER, 2)),
            pltpu.SemaphoreType.DMA((STAGES, PER, 2)),
            pltpu.VMEM((part, slab, size_y), F32),
            pltpu.VMEM((slab, cols, size_y), F32),
            pltpu.SemaphoreType.DMA((PIECES,)),
        ],
        compiler_params=pltpu.CompilerParams(
            collective_id=0, has_side_effects=True, vmem_limit_bytes=56 * 2**20
        ),
        name="deconvolve",
    )(
        observed,
        kernel_x.reshape(1, -1), kernel_y.reshape(1, -1), kernel_z.reshape(1, -1),
    )
    return pl.pallas_call(
        hand_over,
        out_shape=jax.ShapeDtypeStruct(out.shape, F32),
        in_specs=[pl.BlockSpec(memory_space=pltpu.VMEM)],
        out_specs=pl.BlockSpec(memory_space=pl.ANY),
        scratch_shapes=[pltpu.SemaphoreType.DMA((4,))],
        compiler_params=pltpu.CompilerParams(vmem_limit_bytes=8 * 2**20),
        name="hand_over",
    )(out)


def hand_over(src_ref, dst_ref, sem):
    n = src_ref.shape[0] // 4
    copies = [
        pltpu.make_async_copy(src_ref.at[pl.ds(k * n, n)], dst_ref.at[pl.ds(k * n, n)], sem.at[k])
        for k in range(4)
    ]
    for copy in copies:
        copy.start()
    for copy in copies:
        copy.wait()


def solution(mesh):
    return jax.shard_map(
        functools.partial(shards, mesh.shape["zg"], mesh.shape["gx"]),
        mesh=mesh,
        in_specs=(P("zg", "gx", None), P(), P(), P()),
        out_specs=P("zg", "gx", None),
        check_vma=False,
    )
```
